32 devices in a mesh: seq: 16 (over z, y, core), col: 2 (over x).
Axes of the slice: x: 2, y: 2, z: 4, core: 2. Of those that a mesh axis runs over, the one named last changes fastest.
Arguments:
- tokens: bfloat16 [16384, 512], P('seq', 'col'), may hold values from -50 to 50
- cotangent: bfloat16 [16384, 512], P('seq', 'col'), may hold values from -6 to 6
- weight_in: bfloat16 [512, 4, 4, 128], P(None, None, 'col'), may hold values from -0.25 to 0.25
- weight_out: bfloat16 [4, 128, 512], P('col'), may hold values from -0.25 to 0.25
- history_ids: int32 [16384], replicated, may hold values from 0 to 7, never falling along the last dimension, each value on 1 to 4096 neighbouring positions
Outputs:
- out: bfloat16 [16384, 512], P('seq', 'col')
- grad_tokens: bfloat16 [16384, 512], P('seq', 'col')
- grad_weight_in: float32 [512, 4, 4, 128], P(None, None, 'col')
- grad_weight_out: float32 [4, 128, 512], P('col')
The draws below stay inside these ranges and needn't reach their ends.
Inputs may be any that keep to these rules, and one draw needn't show every extreme that they name: history_ids never fall along the stream; every id occurs; each history holds 1 to 4096 tokens and one holds exactly 4096.
All inputs are finite; a program needn't handle non-finite values.
Results may differ from the reference program's by a relative error of at most 0.0092.
Values may be sent and summed in bfloat16 or wider, within the bound.
No kernel may reach another device: no remote copies, remote signals or barrier semaphores. Data moves between devices by JAX's collectives and lax.ppermute only.
A program may use at most 192 MiB of HBM per device.

```python
import math
import jax
import jax.numpy as jnp
import numpy as np
from jax import lax

D = 512
HEADS = 4
HEAD = 128
MAXLEN = 4096
TOKENS = 16384
HISTS = 8


def draw_tokens(key, part):
    first, second, third = jax.random.split(jax.random.fold_in(key, 11), 3)
    row_factor = jnp.exp(jax.random.uniform(second, (TOKENS, 1), jnp.float32, 0.0, jnp.log(10.0))) / jnp.sqrt(10.0)
    col_factor = jnp.exp(jax.random.uniform(third, (1, D), jnp.float32, 0.0, jnp.log(10.0))) / jnp.sqrt(10.0)
    base = jax.random.truncated_normal(first, -4.0, 4.0, (TOKENS, D), jnp.float32)
    return (base * row_factor * col_factor).astype(jnp.bfloat16)


def shard_levels(key, extent, shards, smallest, high):
    gain = 1.0
    for position, blocks in shards:
        steps = jax.random.uniform(jax.random.fold_in(jax.random.fold_in(key, 6), position), (blocks,), jnp.float32, smallest / len(shards), high / len(shards))
        gain = gain * jnp.repeat(jnp.exp(steps), extent[position] // blocks).reshape((-1,) + (1,) * (len(extent) - 1 - position))
    return gain


def profile(number_of, total, bound, slope):
    loads = [(1 << 20) // math.isqrt(standing ** slope) + 1 for standing in range(2, number_of + 1)]
    spare, counts = total - bound - (number_of - 1), [1] * (number_of - 1)
    while spare > 0:
        free = [i for i in range(number_of - 1) if counts[i] < bound]
        whole, left = sum([loads[i] for i in free]), spare
        for i in free:
            extra = min(bound - counts[i], max(1, left * loads[i] // whole), spare)
            counts[i] = counts[i] + extra
            spare = spare - extra
    return np.array([bound] + counts)


def ragged_sizes(key, number_of, total, reach, lean):
    if number_of == 2:
        one = jax.random.randint(key, (), max(1, total - reach), min(reach, total - 1) + 1)
        return jnp.stack([one, total - one])
    lengths = jnp.asarray(profile(number_of, total, reach, lean), jnp.int32)
    pairs = (number_of - 1) // 2
    source_of, taker = lengths[1:1 + 2 * pairs:2], lengths[2:2 + 2 * pairs:2]
    slack = jnp.minimum(source_of - 1, reach - taker)
    moved = jax.random.randint(jax.random.fold_in(key, 1), (pairs,), 0, 1 << 20) % (slack + 1)
    lengths = lengths.at[1:1 + 2 * pairs:2].set(source_of - moved).at[2:2 + 2 * pairs:2].set(taker + moved)
    return lengths[jax.random.permutation(jax.random.fold_in(key, 2), number_of)]


def normal_values(stream_key, shape, scale, bound, cuts=(), held_as=jnp.bfloat16):
    drawn = scale * jax.random.normal(stream_key, shape, jnp.float32)
    if cuts:
        drawn = drawn * shard_levels(stream_key, shape, cuts, -0.22, 0.18)
    return jnp.clip(drawn, -bound, bound).astype(held_as)


def setup_inputs(seed: int = 0) -> dict:
    seeds = jax.random.split(jax.random.key(seed), 6)
    tokens = draw_tokens(jax.random.fold_in(seeds[5], 71), 0)
    cotangent = normal_values(seeds[1], (TOKENS, D), 1.0, 6.0, ((0, 16), (1, 2)))
    weight_in = normal_values(seeds[2], (D, 4, HEADS, HEAD), D ** -0.5, 0.25, ((2, 2),))
    weight_out = normal_values(seeds[3], (HEADS, HEAD, D), D ** -0.5, 0.25, ((0, 2),))
    history_ids = jnp.searchsorted(jnp.cumsum(ragged_sizes(seeds[4], HISTS, TOKENS, MAXLEN, 2)), jnp.arange(TOKENS), side="right").astype(jnp.int32)
    return dict(tokens=tokens, cotangent=cotangent, weight_in=weight_in, weight_out=weight_out, history_ids=history_ids)


epsilon = 1e-05
head_floor = 1.0

def layer_norm(values, offset):
    center = values - lax.optimization_barrier(jnp.mean(values, axis=-1, keepdims=True))
    inv_std = lax.rsqrt(lax.optimization_barrier(jnp.mean(center * center, axis=-1, keepdims=True)) + offset)
    return (center * inv_std, inv_std)

def silu_slope(inputs):
    gate_value = jax.nn.sigmoid(inputs)
    return gate_value * (1.0 + inputs * (1.0 - gate_value))

def norm_back(grad_in, normed, inv_std):
    return inv_std * (grad_in - lax.optimization_barrier(jnp.mean(grad_in, axis=-1, keepdims=True)) - normed * lax.optimization_barrier(jnp.mean(grad_in * normed, axis=-1, keepdims=True)))

def narrow(values):
    return lax.optimization_barrier(values.astype(jnp.bfloat16)).astype(jnp.float32)

def reference(tokens, cotangent, weight_in, weight_out, history_ids):
    block_rows = math.gcd(TOKENS, 512)
    reach_back = (MAXLEN - 1 + block_rows - 1) // block_rows * block_rows
    key_window = min(reach_back + block_rows, TOKENS)
    block_count = TOKENS // block_rows
    score_scale = HEAD ** (-0.5)
    features = tokens.astype(jnp.float32)
    normed, inv_std = layer_norm(features, epsilon)
    normed_b = narrow(normed)
    pre_act = jnp.einsum('td,dphe->tphe', normed_b, weight_in.astype(jnp.float32))
    project = narrow(jax.nn.silu(pre_act))
    up_part = project[:, 0]
    value_part = project[:, 1]
    query_part = project[:, 2]
    key_part = project[:, 3]

    def pieces(block_index):
        q_start = (block_index * block_rows).astype(jnp.int32)
        k_start = jnp.clip(q_start + block_rows - key_window, 0, TOKENS - key_window).astype(jnp.int32)
        query_block = lax.dynamic_slice_in_dim(query_part, q_start, block_rows)
        key_block = lax.dynamic_slice_in_dim(key_part, k_start, key_window)
        value_block = lax.dynamic_slice_in_dim(value_part, k_start, key_window)
        ids_query = lax.dynamic_slice_in_dim(history_ids, q_start, block_rows)
        ids_key = lax.dynamic_slice_in_dim(history_ids, k_start, key_window)
        pos_query = q_start + jnp.arange(block_rows, dtype=jnp.int32)
        pos_key = k_start + jnp.arange(key_window, dtype=jnp.int32)
        allowed = ((ids_query[:, None] == ids_key[None, :]) & (pos_key[None, :] <= pos_query[:, None])).astype(jnp.float32)
        scores = score_scale * jnp.einsum('ihe,jhe->hij', query_block, key_block)
        weights_att = narrow(jax.nn.silu(scores) * allowed[None])
        return (q_start, k_start, query_block, key_block, value_block, allowed, scores, weights_att)

    def forward_block(block_index):
        parts = pieces(block_index)
        return jnp.einsum('hij,jhe->ihe', parts[7], parts[4])
    attended = lax.map(forward_block, jnp.arange(block_count, dtype=jnp.int32)).reshape(TOKENS, HEADS, HEAD)
    head_normed, head_scale = layer_norm(attended, head_floor)
    gated = narrow(head_normed * up_part)
    out_part = jnp.einsum('the,hed->td', gated, weight_out.astype(jnp.float32))
    out = (features + out_part).astype(jnp.bfloat16)
    grad_full = cotangent.astype(jnp.float32)
    grad_gated = jnp.einsum('td,hed->the', grad_full, weight_out.astype(jnp.float32))
    grad_up = grad_gated * head_normed
    grad_heads = norm_back(grad_gated * up_part, head_normed, head_scale)
    grad_narrow = narrow(grad_heads)

    def backward_block(sums_carry, block_index):
        grad_key, grad_value = sums_carry
        q_start, k_start, query_block, key_block, value_block, allowed, scores, weights_att = pieces(block_index)
        grad_block = lax.dynamic_slice_in_dim(grad_narrow, q_start, block_rows)
        grad_scores = narrow(score_scale * allowed[None] * silu_slope(scores) * jnp.einsum('ihe,jhe->hij', grad_block, value_block))
        grad_query = jnp.einsum('hij,jhe->ihe', grad_scores, key_block)
        key_add = jnp.einsum('hij,ihe->jhe', grad_scores, query_block)
        value_add = jnp.einsum('hij,ihe->jhe', weights_att, grad_block)
        grad_key = lax.dynamic_update_slice_in_dim(grad_key, lax.dynamic_slice_in_dim(grad_key, k_start, key_window) + key_add, k_start, 0)
        grad_value = lax.dynamic_update_slice_in_dim(grad_value, lax.dynamic_slice_in_dim(grad_value, k_start, key_window) + value_add, k_start, 0)
        return ((grad_key, grad_value), grad_query)
    empty_grad = jnp.zeros((TOKENS, HEADS, HEAD), jnp.float32)
    (grad_key, grad_value), grad_query = lax.scan(backward_block, (empty_grad, empty_grad), jnp.arange(block_count, dtype=jnp.int32))
    grad_query = grad_query.reshape(TOKENS, HEADS, HEAD)
    grad_proj = jnp.stack([grad_up, grad_value, grad_query, grad_key], axis=1)
    grad_pre = narrow(grad_proj * silu_slope(pre_act))
    inv_root = 1.0 / math.sqrt(TOKENS)
    grad_weight_in = jnp.einsum('td,tphe->dphe', normed_b, grad_pre) * inv_root
    grad_weight_out = jnp.einsum('the,td->hed', gated, grad_full) * inv_root
    grad_normed = jnp.einsum('tphe,dphe->td', grad_pre, weight_in.astype(jnp.float32))
    grad_tokens = (norm_back(grad_normed, normed, inv_std) + grad_full).astype(jnp.bfloat16)
    return (out, grad_tokens, grad_weight_in, grad_weight_out)
```

```python
import math

import jax
import jax.numpy as jnp
from jax import lax
from jax.experimental import pallas as pl
from jax.experimental.pallas import tpu as pltpu
from jax.sharding import PartitionSpec as P

MAXLEN = 4096
TILE = 512

epsilon = 1e-05
head_floor = 1.0
f32 = jnp.float32
bf16 = jnp.bfloat16


def swap(block, axis, bit):
    return lax.ppermute(block, axis, [(i, i ^ bit) for i in range(lax.axis_size(axis))])


def shift(block, axis, distance):
    devices = range(lax.axis_size(axis))
    return lax.ppermute(block, axis, [(i, i + distance) for i in devices if i + distance in devices])


def silu_slope(inputs):
    gate_value = jax.nn.sigmoid(inputs)
    return gate_value * (1.0 + inputs * (1.0 - gate_value))


def layer_norm(values, offset):
    center = values - jnp.mean(values, axis=-1, keepdims=True)
    inv_std = lax.rsqrt(jnp.mean(center * center, axis=-1, keepdims=True) + offset)
    return (center * inv_std, inv_std)


def norm_back(grad_in, normed, inv_std):
    return inv_std * (
        grad_in
        - jnp.mean(grad_in, axis=-1, keepdims=True)
        - normed * jnp.mean(grad_in * normed, axis=-1, keepdims=True)
    )


def tile_span(i, low_ref, block_off, key_tiles, query_off):
    start = jnp.maximum(low_ref[i] - block_off, 0)
    stop = jnp.minimum(query_off + i + 1 - block_off, key_tiles)
    return start, stop


def forward_kernel(low_ref, first_ref, last_ref, q_ref, k_ref, v_ref, idq_ref, idk_ref, *rest, block_off, query_off, scale):
    out_ref = rest[-1]
    q_tiles = q_ref.shape[0] // TILE
    k_tiles = k_ref.shape[0] // TILE
    if len(rest) == 2:
        out_ref[...] = rest[0][...]
    else:
        out_ref[...] = jnp.zeros(out_ref.shape, f32)

    def query_tile(i, carry):
        start, stop = tile_span(i, low_ref, block_off, k_tiles, query_off)
        rows = pl.ds(pl.multiple_of(i * TILE, TILE), TILE)

        def key_tile(j, inner):
            cols = pl.ds(pl.multiple_of(j * TILE, TILE), TILE)
            near = query_off + i - block_off - j
            whole = (near > 0) & (first_ref[block_off + j] == last_ref[query_off + i])

            def step(masked):
                half = lax.dot_general(q_ref[rows, :], k_ref[cols, :], (((1,), (1,)), ((), ())), preferred_element_type=f32)
                half = half * (0.5 * scale)
                weights = half + half * jnp.tanh(half)
                if masked:
                    pos_q = lax.broadcasted_iota(jnp.int32, (TILE, TILE), 0)
                    pos_k = lax.broadcasted_iota(jnp.int32, (TILE, TILE), 1)
                    ok = (idq_ref[rows, :] == idk_ref[:, cols]) & (pos_k - pos_q <= near * TILE)
                    weights = jnp.where(ok, weights, 0.0)
                out_ref[rows, :] += jnp.dot(weights.astype(bf16), v_ref[cols, :], preferred_element_type=f32)

            @pl.when(whole)
            def _():
                step(False)

            @pl.when(jnp.logical_not(whole))
            def _():
                step(True)

            return inner

        lax.fori_loop(start, stop, key_tile, 0)
        return carry

    lax.fori_loop(0, q_tiles, query_tile, 0)


def backward_kernel(low_ref, first_ref, last_ref, q_ref, g_ref, k_ref, v_ref, idq_ref, idk_ref, *rest, block_off, query_off, scale):
    dq_ref, dk_ref, dv_ref = rest[-3:]
    q_tiles = q_ref.shape[0] // TILE
    k_tiles = k_ref.shape[0] // TILE
    if len(rest) == 4:
        dq_ref[...] = rest[0][...]
    else:
        dq_ref[...] = jnp.zeros(dq_ref.shape, f32)
    dk_ref[...] = jnp.zeros(dk_ref.shape, f32)
    dv_ref[...] = jnp.zeros(dv_ref.shape, f32)

    def query_tile(i, carry):
        start, stop = tile_span(i, low_ref, block_off, k_tiles, query_off)
        rows = pl.ds(pl.multiple_of(i * TILE, TILE), TILE)

        def key_tile(j, inner):
            cols = pl.ds(pl.multiple_of(j * TILE, TILE), TILE)
            near = query_off + i - block_off - j
            whole = (near > 0) & (first_ref[block_off + j] == last_ref[query_off + i])

            def step(masked):
                q = q_ref[rows, :]
                g = g_ref[rows, :]
                k = k_ref[cols, :]
                half = lax.dot_general(k, q, (((1,), (1,)), ((), ())), preferred_element_type=f32)
                half = half * (0.5 * scale)
                tanh = jnp.tanh(half)
                gate = 0.5 + 0.5 * tanh
                weights = half + half * tanh
                slope = gate + weights * (1.0 - gate)
                grad = slope * lax.dot_general(v_ref[cols, :], g, (((1,), (1,)), ((), ())), preferred_element_type=f32)
                if masked:
                    pos_k = lax.broadcasted_iota(jnp.int32, (TILE, TILE), 0)
                    pos_q = lax.broadcasted_iota(jnp.int32, (TILE, TILE), 1)
                    ok = (idk_ref[cols, :] == idq_ref[:, rows]) & (pos_k - pos_q <= near * TILE)
                    weights = jnp.where(ok, weights, 0.0)
                    grad = jnp.where(ok, grad, 0.0)
                grad = grad.astype(bf16)
                dv_ref[cols, :] += jnp.dot(weights.astype(bf16), g, preferred_element_type=f32)
                dk_ref[cols, :] += jnp.dot(grad, q, preferred_element_type=f32)
                dq_ref[rows, :] += lax.dot_general(grad, k, (((0,), (0,)), ((), ())), preferred_element_type=f32)

            @pl.when(whole)
            def _():
                step(False)

            @pl.when(jnp.logical_not(whole))
            def _():
                step(True)

            return inner

        lax.fori_loop(start, stop, key_tile, 0)
        return carry

    lax.fori_loop(0, q_tiles, query_tile, 0)


def vmem_call(kernel, tables, arrays, outs, aliases, **static):
    whole = pl.BlockSpec(memory_space=pltpu.VMEM)
    table = pl.BlockSpec(memory_space=pltpu.SMEM)
    return pl.pallas_call(
        lambda *refs: kernel(*refs, **static),
        out_shape=outs,
        in_specs=[table] * len(tables) + [whole] * len(arrays),
        out_specs=jax.tree.map(lambda _: whole, outs),
        input_output_aliases=aliases,
        compiler_params=pltpu.CompilerParams(vmem_limit_bytes=60 << 20),
    )(*tables, *arrays)


def shards(tokens, cotangent, weight_in, weight_out, history_ids):
    row_count, half_width = tokens.shape
    seq_count = lax.axis_size("seq")
    device_pos = lax.axis_index("seq")
    core = device_pos % 2
    pair = device_pos // 2
    odd = pair % 2 == 1
    block = 2 * row_count
    head_size = weight_out.shape[1]
    scale = head_size ** (-0.5)
    if (MAXLEN - 2 + block) // block != 2:
        raise ValueError("reach")
    tiles = block // TILE

    far_half = shift(tokens, "seq", 4)
    own_other = swap(tokens, "col", 1)
    near_half = swap(jnp.where(odd, far_half, tokens), "seq", 2)

    def gathered(mine, other):
        wide = jnp.concatenate([mine, other], axis=1)
        partner = swap(wide, "seq", 1)
        return jnp.where(
            core == 0, jnp.concatenate([wide, partner], axis=0), jnp.concatenate([partner, wide], axis=0)
        )

    own_tokens = gathered(tokens, own_other)
    far_tokens = gathered(far_half, swap(far_half, "col", 1))
    near_tokens = gathered(near_half, swap(near_half, "col", 1))
    grad_full = gathered(cotangent, swap(cotangent, "col", 1))

    flip = lax.axis_index("col") == 1
    w_in = lax.dynamic_index_in_dim(weight_in, core, 2, keepdims=False)
    w_in = jnp.where(flip, jnp.roll(w_in, half_width, axis=0), w_in)
    w_out = lax.dynamic_index_in_dim(weight_out, core, 0, keepdims=False)
    w_out = jnp.where(flip, jnp.roll(w_out, half_width, axis=1), w_out)
    w_all = w_in.reshape(2 * half_width, 4 * head_size)
    w_kv = jnp.concatenate([w_in[:, 1], w_in[:, 3]], axis=1)

    padded = jnp.concatenate([jnp.full((2 * block,), -1, jnp.int32), history_ids])
    ids = lax.dynamic_slice_in_dim(padded, pair * block, 3 * block)
    by_tile = ids.reshape(-1, TILE)
    first, last = by_tile[:, 0], by_tile[:, -1]
    low = jnp.sum((last[None, :] < first[2 * tiles :, None]).astype(jnp.int32), axis=1)
    tables = (low, first, last)
    own_ids = ids[2 * block :]

    def project(values, weights):
        normed, inv_std = layer_norm(values.astype(f32), epsilon)
        normed_b = normed.astype(bf16)
        pre_act = jnp.dot(normed_b, weights, preferred_element_type=f32)
        return normed_b, pre_act, jax.nn.silu(pre_act).astype(bf16)

    normed_own, pre_own, part_own = project(own_tokens, w_all)
    up_part, value_own, query, key_own = jnp.split(part_own, 4, axis=1)
    normed_far, pre_far, part_far = project(far_tokens, w_kv)
    normed_near, pre_near, part_near = project(near_tokens, w_kv)
    keys = [part_far[:, head_size:], part_near[:, head_size:], key_own]
    values = [part_far[:, :head_size], part_near[:, :head_size], value_own]

    def forward(which, before):
        span = slice(which * block, (which + 1) * block)
        arrays = [query, keys[which], values[which], own_ids[:, None], ids[None, span]]
        aliases = {}
        if before is not None:
            aliases = {3 + len(arrays): 0}
            arrays.append(before)
        return vmem_call(
            forward_kernel,
            tables,
            arrays,
            jax.ShapeDtypeStruct((block, head_size), f32),
            aliases,
            block_off=which * tiles,
            query_off=2 * tiles,
            scale=scale,
        )

    attended = forward(1, forward(0, forward(2, None)))

    head_normed, head_scale = layer_norm(attended, head_floor)
    up_wide = up_part.astype(f32)
    gated = (head_normed * up_wide).astype(bf16)
    grad_gated = lax.dot_general(grad_full, w_out, (((1,), (1,)), ((), ())), preferred_element_type=f32)
    grad_up = grad_gated * head_normed
    grad_narrow = norm_back(grad_gated * up_wide, head_normed, head_scale).astype(bf16)

    def rows_of(array, which):
        return lax.dynamic_slice_in_dim(array, which * row_count, row_count)

    def over_heads(narrow_rows, weights):
        sent = jnp.dot(rows_of(narrow_rows, 1 - core), weights, preferred_element_type=f32).astype(bf16)
        kept = jnp.dot(rows_of(narrow_rows, core), weights, preferred_element_type=f32)
        kept = kept + swap(sent, "seq", 1).astype(f32)
        return kept[:, :half_width] + swap(kept[:, half_width:].astype(bf16), "col", 1).astype(f32)

    out = (tokens.astype(f32) + over_heads(gated, w_out)).astype(bf16)

    bits = []
    while 2 << len(bits) < seq_count:
        bits.append(2 << len(bits))

    def sum_over_seq(array):
        for bit in bits:
            size = array.shape[0] // 2
            high = (device_pos & bit) // bit
            sent = lax.dynamic_slice_in_dim(array, (1 - high) * size, size).astype(bf16)
            array = lax.dynamic_slice_in_dim(array, high * size, size) + swap(sent, "seq", bit).astype(f32)
        array = array.astype(bf16)
        for bit in reversed(bits):
            other = swap(array, "seq", bit)
            array = jnp.where(
                (device_pos & bit) != 0,
                jnp.concatenate([other, array], axis=0),
                jnp.concatenate([array, other], axis=0),
            )
        return array

    def weight_grad(normed, grads):
        return lax.dot_general(normed, grads, (((0,), (0,)), ((), ())), preferred_element_type=f32)

    pre_up = pre_own[:, :head_size]
    grad_pre_up = (grad_up * silu_slope(pre_up)).astype(bf16)
    grad_w_up = weight_grad(normed_own, grad_pre_up)
    grad_w_out = weight_grad(gated, grad_full)
    early = sum_over_seq(jnp.concatenate([grad_w_up, grad_w_out.reshape(-1, head_size)], axis=0))

    def backward(which, before):
        span = slice(which * block, (which + 1) * block)
        arrays = [query, grad_narrow, keys[which], values[which], own_ids[None, :], ids[span, None]]
        aliases = {}
        if before is not None:
            aliases = {3 + len(arrays): 0}
            arrays.append(before)
        shape = jax.ShapeDtypeStruct((block, head_size), f32)
        return vmem_call(
            backward_kernel,
            tables,
            arrays,
            (shape, shape, shape),
            aliases,
            block_off=which * tiles,
            query_off=2 * tiles,
            scale=scale,
        )

    grad_query, dk_near, dv_near = backward(1, None)
    w_kv_t = w_kv.T

    def halo(dk, dv, pre, normed):
        grads = jnp.concatenate([dv, dk * scale], axis=1)
        grads = (grads * silu_slope(pre)).astype(bf16)
        return over_heads(grads, w_kv_t), weight_grad(normed, grads)

    near_part, near_w = halo(dk_near, dv_near, pre_near, normed_near)
    near_back = swap(near_part.astype(bf16), "seq", 2).astype(f32)
    grad_query, dk_far, dv_far = backward(0, grad_query)
    far_part, far_w = halo(dk_far, dv_far, pre_far, normed_far)
    far_part = far_part + jnp.where(odd, near_back, 0.0)
    far_back = shift(far_part.astype(bf16), "seq", -4).astype(f32)
    grad_query, dk_own, dv_own = backward(2, grad_query)
    own_grads = jnp.concatenate([dv_own, grad_query * scale, dk_own * scale], axis=1)
    own_grads = (own_grads * silu_slope(pre_own[:, head_size:])).astype(bf16)
    own_w = weight_grad(normed_own, own_grads)
    own_grads = jnp.concatenate([grad_pre_up, own_grads], axis=1)
    own_part = over_heads(own_grads, w_all.T)
    grad_normed = own_part + jnp.where(odd, 0.0, near_back) + far_back

    late = jnp.concatenate(
        [
            own_w[:, :head_size] + near_w[:, :head_size] + far_w[:, :head_size],
            own_w[:, head_size : 2 * head_size],
            own_w[:, 2 * head_size :] + near_w[:, head_size:] + far_w[:, head_size:],
        ],
        axis=0,
    )
    late = sum_over_seq(late)

    inv_root = 1.0 / math.sqrt(row_count * seq_count)
    width = 2 * half_width
    parts = jnp.concatenate([early[:width], late], axis=0).reshape(4, width, head_size)
    both = jnp.stack([parts.reshape(4 * width, head_size), swap(parts.reshape(4 * width, head_size), "seq", 1)])
    both = jnp.where(core == 0, both, both[::-1]).reshape(2, 4, width, head_size)
    both = jnp.where(flip, jnp.roll(both, half_width, axis=2), both)
    grad_weight_in = both.transpose(2, 1, 0, 3).astype(f32) * inv_root
    mine = early[width:].reshape(head_size, width)
    mine = jnp.where(flip, jnp.roll(mine, half_width, axis=1), mine)
    outs = jnp.stack([mine, swap(mine, "seq", 1)])
    grad_weight_out = jnp.where(core == 0, outs, outs[::-1]).astype(f32) * inv_root

    own_wide = jnp.concatenate([tokens, own_other], axis=1).astype(f32)
    normed, inv_std = layer_norm(own_wide, epsilon)
    normed = normed[:, :half_width]
    sums = jnp.stack([jnp.sum(grad_normed, axis=1), jnp.sum(grad_normed * normed, axis=1)])
    sums = (sums + swap(sums, "col", 1)) / width
    grad_tokens = inv_std * (grad_normed - sums[0][:, None] - normed * sums[1][:, None])
    grad_tokens = (grad_tokens + cotangent.astype(f32)).astype(bf16)
    return (out, grad_tokens, grad_weight_in, grad_weight_out)


def solution(mesh):
    placed = (
        P("seq", "col"),
        P("seq", "col"),
        P(None, None, "col", None),
        P("col", None, None),
        P(),
    )
    return jax.shard_map(
        shards,
        mesh=mesh,
        in_specs=placed,
        out_specs=(
            P("seq", "col"),
            P("seq", "col"),
            P(None, None, "col", None),
            P("col", None, None),
        ),
        check_vma=False,
    )
```

```python
import math

import jax
import jax.numpy as jnp
from jax import lax
from jax.experimental import pallas as pl
from jax.experimental.pallas import tpu as pltpu
from jax.sharding import PartitionSpec as P

MAXLEN = 4096
TILE = 512

epsilon = 1e-05
head_floor = 1.0
f32 = jnp.float32
bf16 = jnp.bfloat16


def swap(block, axis, bit):
    return lax.ppermute(block, axis, [(i, i ^ bit) for i in range(lax.axis_size(axis))])


def shift(block, axis, distance):
    devices = range(lax.axis_size(axis))
    return lax.ppermute(block, axis, [(i, i + distance) for i in devices if i + distance in devices])


def layer_norm(values, offset):
    center = values - jnp.mean(values, axis=-1, keepdims=True)
    inv_std = lax.rsqrt(jnp.mean(center * center, axis=-1, keepdims=True) + offset)
    return (center * inv_std, inv_std)


def norm_back(grad_in, normed, inv_std):
    return inv_std * (
        grad_in
        - jnp.mean(grad_in, axis=-1, keepdims=True)
        - normed * jnp.mean(grad_in * normed, axis=-1, keepdims=True)
    )


NT = (((1,), (1,)), ((), ()))
TN = (((0,), (0,)), ((), ()))


def dot(a, b, dims=(((1,), (0,)), ((), ()))):
    return lax.dot_general(a, b, dims, preferred_element_type=f32)


def gate_of(inputs):
    return 0.5 + 0.5 * jnp.tanh(0.5 * inputs)


def aligned(start, size):
    return pl.ds(pl.multiple_of(start, size), size)


def project_kernel(core_ref, mine_a, mine_b, other_a, other_b, w_ref, normed_ref, slope_ref, *part_refs):
    size = 256
    count = mine_a.shape[0]
    core = core_ref[0]
    for first, second, where in ((mine_a, mine_b, core), (other_a, other_b, 1 - core)):

        def rows_step(step, carry, first=first, second=second, where=where):
            rows = aligned(step * size, size)
            into = aligned(where * count + step * size, size)
            values = jnp.concatenate([first[rows, :].astype(f32), second[rows, :].astype(f32)], axis=1)
            normed = layer_norm(values, epsilon)[0].astype(bf16)
            normed_ref[into, :] = normed
            pre = dot(normed, w_ref[...])
            gate = gate_of(pre)
            act = pre * gate
            slope_ref[into, :] = (gate + act * (1.0 - gate)).astype(bf16)
            width = part_refs[0].shape[1]
            for p, part in enumerate(part_refs):
                part[into, :] = act[:, p * width : (p + 1) * width].astype(bf16)
            return carry

        lax.fori_loop(0, count // size, rows_step, 0)


def middle_kernel(core_ref, att_ref, up_ref, slope_ref, mine_a, mine_b, other_a, other_b, w_ref, narrow_ref, gated_ref, pre_up_ref):
    size = 256
    count = mine_a.shape[0]
    half = mine_a.shape[1]
    core = core_ref[0]
    for first, second, where in ((mine_a, mine_b, core), (other_a, other_b, 1 - core)):

        def rows_step(step, carry, first=first, second=second, where=where):
            rows = aligned(step * size, size)
            into = aligned(where * count + step * size, size)
            head_normed, head_scale = layer_norm(att_ref[into, :], head_floor)
            up = up_ref[into, :].astype(f32)
            gated_ref[into, :] = (head_normed * up).astype(bf16)
            grad = dot(first[rows, :], w_ref[:, :half], NT) + dot(second[rows, :], w_ref[:, half:], NT)
            pre_up_ref[into, :] = (grad * head_normed * slope_ref[into, :].astype(f32)).astype(bf16)
            narrow_ref[into, :] = norm_back(grad * up, head_normed, head_scale).astype(bf16)
            return carry

        lax.fori_loop(0, count // size, rows_step, 0)


def outer_kernel(core_ref, gated_ref, pre_up_ref, normed_ref, mine_a, mine_b, other_a, other_b, w_ref, send_ref, keep_ref, grad_ref):
    count, half = mine_a.shape
    width = gated_ref.shape[1]
    core = core_ref[0]
    mine = aligned(core * count, count)
    other = aligned((1 - core) * count, count)
    send_ref[...] = dot(gated_ref[other, :], w_ref[...]).astype(bf16)
    keep_ref[...] = dot(gated_ref[mine, :], w_ref[...]).astype(bf16)
    grad_ref[:, :width] = dot(normed_ref[...], pre_up_ref[...], TN)
    grad_ref[:half, width:] = dot(mine_a[...], gated_ref[mine, :], TN) + dot(other_a[...], gated_ref[other, :], TN)
    grad_ref[half:, width:] = dot(mine_b[...], gated_ref[mine, :], TN) + dot(other_b[...], gated_ref[other, :], TN)


def for_tiles(low_ref, first_ref, last_ref, q_tiles, k_tiles, block_off, query_off, step):
    def query_tile(i, carry):
        start = jnp.maximum(low_ref[i] - block_off, 0)
        stop = jnp.minimum(query_off + i + 1 - block_off, k_tiles)
        rows = aligned(i * TILE, TILE)

        def key_tile(j, inner):
            cols = aligned(j * TILE, TILE)
            near = query_off + i - block_off - j
            whole = (near > 0) & (first_ref[block_off + j] == last_ref[query_off + i])

            @pl.when(whole)
            def _():
                step(rows, cols, None)

            @pl.when(jnp.logical_not(whole))
            def _():
                step(rows, cols, near * TILE)

            return inner

        lax.fori_loop(start, stop, key_tile, 0)
        return carry

    lax.fori_loop(0, q_tiles, query_tile, 0)


def forward_kernel(low_ref, first_ref, last_ref, q_ref, k_ref, v_ref, idq_ref, idk_ref, *rest, block_off, query_off, scale):
    out_ref = rest[-1]
    if len(rest) == 2:
        out_ref[...] = rest[0][...]
    else:
        out_ref[...] = jnp.zeros(out_ref.shape, f32)

    def step(rows, cols, reach):
        half = dot(q_ref[rows, :], k_ref[cols, :], NT) * (0.5 * scale)
        if reach is not None:
            pos_q = lax.broadcasted_iota(jnp.int32, (TILE, TILE), 0)
            pos_k = lax.broadcasted_iota(jnp.int32, (TILE, TILE), 1)
            ok = (idq_ref[rows, :] == idk_ref[:, cols]) & (pos_k - pos_q <= reach)
            half = jnp.where(ok, half, 0.0)
        weights = half + half * jnp.tanh(half)
        out_ref[rows, :] += dot(weights.astype(bf16), v_ref[cols, :])

    for_tiles(
        low_ref, first_ref, last_ref, q_ref.shape[0] // TILE, k_ref.shape[0] // TILE, block_off, query_off, step
    )


def backward_kernel(low_ref, first_ref, last_ref, core_ref, q_ref, g_ref, k_ref, v_ref, idq_ref, idk_ref, w_ref, slope_hbm, normed_hbm, *rest, block_off, query_off, scale, count_in):
    before = rest[:count_in]
    send_ref, keep_ref, grad_ref = rest[count_in : count_in + 3]
    if block_off != query_off:
        dq_ref = rest[count_in + 3]
    else:
        dq_ref = rest[-6]
    dk_ref, dv_ref, slope_ref, normed_ref, sems = rest[-5:]
    q_tiles = q_ref.shape[0] // TILE
    k_tiles = k_ref.shape[0] // TILE
    own = block_off == query_off
    slope_copy = pltpu.make_async_copy(slope_hbm, slope_ref, sems.at[0])
    normed_copy = pltpu.make_async_copy(normed_hbm, normed_ref, sems.at[1])
    slope_copy.start()
    normed_copy.start()
    width = k_ref.shape[1]
    if len(before) > 0:
        dq_ref[...] = before[0][...]
    else:
        dq_ref[...] = jnp.zeros(dq_ref.shape, f32)
    dk_ref[...] = jnp.zeros(dk_ref.shape, f32)
    dv_ref[...] = jnp.zeros(dv_ref.shape, f32)

    def step(rows, cols, reach):
        q = q_ref[rows, :]
        g = g_ref[rows, :]
        k = k_ref[cols, :]
        half = dot(k, q, NT) * (0.5 * scale)
        grad = dot(v_ref[cols, :], g, NT)
        if reach is not None:
            pos_k = lax.broadcasted_iota(jnp.int32, (TILE, TILE), 0)
            pos_q = lax.broadcasted_iota(jnp.int32, (TILE, TILE), 1)
            ok = (idk_ref[cols, :] == idq_ref[:, rows]) & (pos_k - pos_q <= reach)
            half = jnp.where(ok, half, 0.0)
            grad = jnp.where(ok, grad, 0.0)
        twice = (1.0 + jnp.tanh(half)).astype(bf16)
        weights = half.astype(bf16) * twice
        gate = twice * bf16(0.5)
        grad = (gate + weights * (bf16(1.0) - gate)) * grad.astype(bf16)
        dv_ref[cols, :] += dot(weights, g)
        dk_ref[cols, :] += dot(grad, q)
        dq_ref[rows, :] += dot(grad, k, TN)

    for_tiles(low_ref, first_ref, last_ref, q_tiles, k_tiles, block_off, query_off, step)
    slope_copy.wait()
    normed_copy.wait()
    core = core_ref[0]
    count = send_ref.shape[0]
    base = width if own else 0

    def narrow(grads, part):
        into = slope_ref.at[:, part * width : (part + 1) * width]
        into[...] = (grads * into[...].astype(f32)).astype(bf16)

    if own:
        slope_ref[:, :width] = before[-1][...]
        narrow(dv_ref[...], 1)
        narrow(dq_ref[...] * scale, 2)
        narrow(dk_ref[...] * scale, 3)
    else:
        narrow(dv_ref[...], 0)
        narrow(dk_ref[...] * scale, 1)
    send_ref[...] = dot(slope_ref[aligned((1 - core) * count, count), :], w_ref[...], NT).astype(bf16)
    keep_ref[...] = dot(slope_ref[aligned(core * count, count), :], w_ref[...], NT).astype(bf16)
    grads = dot(normed_ref[...], slope_ref[:, base:], TN)
    if own:
        grad_ref[:, :width] = grads[:, :width] + before[1][:, :width]
        grad_ref[:, width : 2 * width] = grads[:, width : 2 * width]
        grad_ref[:, 2 * width :] = grads[:, 2 * width :] + before[1][:, width:]
    elif len(before) > 1:
        grad_ref[...] = grads + before[1][...]
    else:
        grad_ref[...] = grads


def vmem_call(kernel, tables, arrays, outs, aliases=None, hbm=(), scratch=(), **static):
    whole = pl.BlockSpec(memory_space=pltpu.VMEM)
    table = pl.BlockSpec(memory_space=pltpu.SMEM)
    place = [pl.BlockSpec(memory_space=pl.ANY) if i in hbm else whole for i in range(len(arrays))]
    return pl.pallas_call(
        lambda *refs: kernel(*refs, **static),
        out_shape=outs,
        in_specs=[table] * len(tables) + place,
        out_specs=jax.tree.map(lambda _: whole, outs),
        input_output_aliases=aliases or {},
        scratch_shapes=list(scratch),
        compiler_params=pltpu.CompilerParams(vmem_limit_bytes=60 << 20),
    )(*tables, *arrays)


def layer(tokens, cotangent, weight_in, weight_out, history_ids):
    row_count, half_width = tokens.shape
    seq_count = lax.axis_size("seq")
    device_pos = lax.axis_index("seq")
    core = device_pos % 2
    pair = device_pos // 2
    odd = pair % 2 == 1
    block = 2 * row_count
    width = 2 * half_width
    head_size = weight_out.shape[1]
    scale = head_size ** (-0.5)
    if (MAXLEN - 2 + block) // block != 2:
        raise ValueError("reach")
    tiles = block // TILE
    core_table = core.astype(jnp.int32).reshape(1)

    def over(array, axis, bit):
        return swap(array, axis, bit)

    far = shift(tokens, "seq", 4)
    own_other = over(tokens, "col", 1)
    own_set = (tokens, own_other, over(tokens, "seq", 1), over(own_other, "seq", 1))
    near = over(jnp.where(odd, far, tokens), "seq", 2)
    far_other = over(far, "col", 1)
    far_set = (far, far_other, over(far, "seq", 1), over(far_other, "seq", 1))
    near_other = over(near, "col", 1)
    near_set = (near, near_other, over(near, "seq", 1), over(near_other, "seq", 1))
    cot_other = over(cotangent, "col", 1)
    cot_set = (cotangent, cot_other, over(cotangent, "seq", 1), over(cot_other, "seq", 1))

    flip = lax.axis_index("col") == 1
    w_in = lax.dynamic_index_in_dim(weight_in, core, 2, keepdims=False).reshape(width, 4 * head_size)
    w_in = jnp.where(flip, jnp.roll(w_in, half_width, axis=0), w_in)
    w_out = lax.dynamic_index_in_dim(weight_out, core, 0, keepdims=False)
    w_out = jnp.where(flip, jnp.roll(w_out, half_width, axis=1), w_out)
    w_kv = jnp.concatenate([w_in[:, head_size : 2 * head_size], w_in[:, 3 * head_size :]], axis=1)

    padded = jnp.concatenate([jnp.full((2 * block,), -1, jnp.int32), history_ids])
    ids = lax.dynamic_slice_in_dim(padded, pair * block, 3 * block)
    by_tile = ids.reshape(-1, TILE)
    first, last = by_tile[:, 0], by_tile[:, -1]
    low = jnp.sum((last[None, :] < first[2 * tiles :, None]).astype(jnp.int32), axis=1)
    tables = (low, first, last)
    own_ids = ids[2 * block :]

    def shape(rows, cols, dtype=bf16):
        return jax.ShapeDtypeStruct((rows, cols), dtype)

    def project(token_set, weights):
        count = weights.shape[1] // head_size
        outs = (shape(block, width), shape(block, count * head_size)) + (shape(block, head_size),) * count
        return vmem_call(project_kernel, (core_table,), (*token_set, weights), outs)

    normed_own, slope_own, up_part, value_own, query, key_own = project(own_set, w_in)
    normed_far, slope_far, value_far, key_far = project(far_set, w_kv)
    normed_near, slope_near, value_near, key_near = project(near_set, w_kv)
    keys = [key_far, key_near, key_own]
    values = [value_far, value_near, value_own]

    def forward(which, before):
        span = slice(which * block, (which + 1) * block)
        arrays = [query, keys[which], values[which], own_ids[:, None], ids[None, span]]
        aliases = {}
        if before is not None:
            aliases = {3 + len(arrays): 0}
            arrays.append(before)
        return vmem_call(
            forward_kernel,
            tables,
            arrays,
            shape(block, head_size, f32),
            aliases,
            block_off=which * tiles,
            query_off=2 * tiles,
            scale=scale,
        )

    attended = forward(2, None)
    attended = forward(0, attended)
    attended = forward(1, attended)

    grad_narrow, gated, pre_up = vmem_call(
        middle_kernel,
        (core_table,),
        (attended, up_part, slope_own[:, :head_size], *cot_set, w_out),
        (shape(block, head_size),) * 3,
    )
    out_send, out_keep, grad_early = vmem_call(
        outer_kernel,
        (core_table,),
        (gated, pre_up, normed_own, *cot_set, w_out),
        (shape(row_count, width), shape(row_count, width), shape(width, 2 * head_size, f32)),
    )

    def over_heads(send, keep):
        keep = keep.astype(f32) + over(send, "seq", 1).astype(f32)
        return keep[:, :half_width] + over(keep[:, half_width:].astype(bf16), "col", 1).astype(f32)

    def backward(which, weights, slope, normed, before):
        span = slice(which * block, (which + 1) * block)
        arrays = [query, grad_narrow, keys[which], values[which], own_ids[None, :], ids[span, None], weights, slope, normed]
        count = weights.shape[1]
        own = which == 2
        grads = count - head_size if own else count
        outs = [shape(row_count, width), shape(row_count, width), shape(width, grads, f32)]
        scratch = [
            pltpu.VMEM((block, head_size), f32),
            pltpu.VMEM((block, head_size), f32),
            pltpu.VMEM((block, count), bf16),
            pltpu.VMEM((block, width), bf16),
            pltpu.SemaphoreType.DMA((2,)),
        ]
        if own:
            scratch = [pltpu.VMEM((block, head_size), f32)] + scratch
        else:
            outs.append(shape(block, head_size, f32))
        return vmem_call(
            backward_kernel,
            (*tables, core_table),
            arrays + list(before),
            tuple(outs),
            hbm=(len(arrays) - 2, len(arrays) - 1),
            scratch=scratch,
            block_off=which * tiles,
            query_off=2 * tiles,
            scale=scale,
            count_in=len(before),
        )

    near_send, near_keep, grad_kv, grad_query = backward(1, w_kv, slope_near, normed_near, ())
    near_part = over_heads(near_send, near_keep)
    near_back = over(near_part.astype(bf16), "seq", 2).astype(f32)
    far_send, far_keep, grad_kv, grad_query = backward(0, w_kv, slope_far, normed_far, (grad_query, grad_kv))
    far_part = over_heads(far_send, far_keep) + jnp.where(odd, near_back, 0.0)
    far_back = shift(far_part.astype(bf16), "seq", -4).astype(f32)
    own_send, own_keep, grad_own = backward(2, w_in, slope_own, normed_own, (grad_query, grad_kv, pre_up))
    own_part = over_heads(own_send, own_keep)
    grad_normed = own_part + jnp.where(odd, 0.0, near_back) + far_back
    out = (tokens.astype(f32) + over_heads(out_send, out_keep)).astype(bf16)

    total = jnp.concatenate([grad_early[:, :head_size], grad_own, grad_early[:, head_size:]], axis=1)
    bits = []
    while 2 << len(bits) < seq_count:
        bits.append(2 << len(bits))
    for bit in bits:
        size = total.shape[0] // 2
        high = (device_pos & bit) // bit
        sent = lax.dynamic_slice_in_dim(total, (1 - high) * size, size).astype(bf16)
        total = lax.dynamic_slice_in_dim(total, high * size, size) + over(sent, "seq", bit).astype(f32)
    total = total.astype(bf16)
    for bit in reversed(bits):
        other = over(total, "seq", bit)
        total = jnp.where(
            (device_pos & bit) != 0,
            jnp.concatenate([other, total], axis=0),
            jnp.concatenate([total, other], axis=0),
        )

    inv_root = 1.0 / math.sqrt(row_count * seq_count)
    total = jnp.where(flip, jnp.roll(total, half_width, axis=0), total)
    both = jnp.stack([total, over(total, "seq", 1)])
    both = jnp.where(core == 0, both, both[::-1])
    grad_weight_in = both[:, :, : 4 * head_size].reshape(2, width, 4, head_size).transpose(1, 2, 0, 3)
    grad_weight_in = grad_weight_in.astype(f32) * inv_root
    grad_weight_out = both[:, :, 4 * head_size :].transpose(0, 2, 1).astype(f32) * inv_root

    own_wide = jnp.concatenate([tokens, own_other], axis=1).astype(f32)
    normed, inv_std = layer_norm(own_wide, epsilon)
    normed = normed[:, :half_width]
    sums = jnp.stack([jnp.sum(grad_normed, axis=1), jnp.sum(grad_normed * normed, axis=1)])
    sums = (sums + over(sums, "col", 1)) / width
    grad_tokens = inv_std * (grad_normed - sums[0][:, None] - normed * sums[1][:, None])
    grad_tokens = (grad_tokens + cotangent.astype(f32)).astype(bf16)
    return (out, grad_tokens, grad_weight_in, grad_weight_out)


def solution(mesh):
    placed = (
        P("seq", "col"),
        P("seq", "col"),
        P(None, None, "col", None),
        P("col", None, None),
        P(),
    )
    return jax.shard_map(
        layer,
        mesh=mesh,
        in_specs=placed,
        out_specs=(
            P("seq", "col"),
            P("seq", "col"),
            P(None, None, "col", None),
            P("col", None, None),
        ),
        check_vma=False,
    )
```

```python
import math

import jax
import jax.numpy as jnp
from jax import lax
from jax.experimental import pallas as pl
from jax.experimental.pallas import tpu as pltpu
from jax.sharding import PartitionSpec as P

MAXLEN = 4096
TILE = 512

epsilon = 1e-05
head_floor = 1.0
f32 = jnp.float32
bf16 = jnp.bfloat16


def swap(block, axis, bit):
    return lax.ppermute(block, axis, [(i, i ^ bit) for i in range(lax.axis_size(axis))])


def shift(block, axis, distance):
    devices = range(lax.axis_size(axis))
    return lax.ppermute(block, axis, [(i, i + distance) for i in devices if i + distance in devices])


def layer_norm(values, offset):
    center = values - jnp.mean(values, axis=-1, keepdims=True)
    inv_std = lax.rsqrt(jnp.mean(center * center, axis=-1, keepdims=True) + offset)
    return (center * inv_std, inv_std)


def norm_back(grad_in, normed, inv_std):
    return inv_std * (
        grad_in
        - jnp.mean(grad_in, axis=-1, keepdims=True)
        - normed * jnp.mean(grad_in * normed, axis=-1, keepdims=True)
    )


NT = (((1,), (1,)), ((), ()))
TN = (((0,), (0,)), ((), ()))


def dot(a, b, dims=(((1,), (0,)), ((), ()))):
    return lax.dot_general(a, b, dims, preferred_element_type=f32)


def gate_of(inputs):
    return 0.5 + 0.5 * jnp.tanh(0.5 * inputs)


def aligned(start, size):
    return pl.ds(pl.multiple_of(start, size), size)


def project_kernel(core_ref, mine_a, mine_b, other_a, other_b, w_ref, normed_ref, slope_ref, *part_refs):
    size = 256
    count = mine_a.shape[0]
    core = core_ref[0]
    for first, second, where in ((mine_a, mine_b, core), (other_a, other_b, 1 - core)):

        def rows_step(step, carry, first=first, second=second, where=where):
            rows = aligned(step * size, size)
            into = aligned(where * count + step * size, size)
            values = jnp.concatenate([first[rows, :].astype(f32), second[rows, :].astype(f32)], axis=1)
            normed = layer_norm(values, epsilon)[0].astype(bf16)
            normed_ref[into, :] = normed
            pre = dot(normed, w_ref[...])
            gate = gate_of(pre)
            act = pre * gate
            slope_ref[into, :] = (gate + act * (1.0 - gate)).astype(bf16)
            width = part_refs[0].shape[1]
            for p, part in enumerate(part_refs):
                part[into, :] = act[:, p * width : (p + 1) * width].astype(bf16)
            return carry

        lax.fori_loop(0, count // size, rows_step, 0)


def middle_kernel(core_ref, att_ref, up_ref, slope_ref, mine_a, mine_b, other_a, other_b, w_ref, narrow_ref, gated_ref, pre_up_ref):
    size = 256
    count = mine_a.shape[0]
    half = mine_a.shape[1]
    core = core_ref[0]
    for first, second, where in ((mine_a, mine_b, core), (other_a, other_b, 1 - core)):

        def rows_step(step, carry, first=first, second=second, where=where):
            rows = aligned(step * size, size)
            into = aligned(where * count + step * size, size)
            head_normed, head_scale = layer_norm(att_ref[into, :], head_floor)
            up = up_ref[into, :].astype(f32)
            gated_ref[into, :] = (head_normed * up).astype(bf16)
            grad = dot(first[rows, :], w_ref[:, :half], NT) + dot(second[rows, :], w_ref[:, half:], NT)
            pre_up_ref[into, :] = (grad * head_normed * slope_ref[into, : up.shape[1]].astype(f32)).astype(bf16)
            narrow_ref[into, :] = norm_back(grad * up, head_normed, head_scale).astype(bf16)
            return carry

        lax.fori_loop(0, count // size, rows_step, 0)


def outer_kernel(core_ref, gated_ref, pre_up_ref, normed_ref, mine_a, mine_b, other_a, other_b, w_ref, send_ref, keep_ref, grad_ref):
    count, half = mine_a.shape
    width = gated_ref.shape[1]
    core = core_ref[0]
    mine = aligned(core * count, count)
    other = aligned((1 - core) * count, count)
    send_ref[...] = dot(gated_ref[other, :], w_ref[...]).astype(bf16)
    keep_ref[...] = dot(gated_ref[mine, :], w_ref[...]).astype(bf16)
    grad_ref[:, :width] = dot(normed_ref[...], pre_up_ref[...], TN)
    grad_ref[:half, width:] = dot(mine_a[...], gated_ref[mine, :], TN) + dot(other_a[...], gated_ref[other, :], TN)
    grad_ref[half:, width:] = dot(mine_b[...], gated_ref[mine, :], TN) + dot(other_b[...], gated_ref[other, :], TN)


def for_tiles(low_ref, first_ref, last_ref, q_tiles, k_tiles, block_off, query_off, step):
    def query_tile(i, carry):
        start = jnp.maximum(low_ref[i] - block_off, 0)
        stop = jnp.minimum(query_off + i + 1 - block_off, k_tiles)

        def key_tile(j, inner):
            near = query_off + i - block_off - j
            whole = (near > 0) & (first_ref[block_off + j] == last_ref[query_off + i])

            @pl.when(whole)
            def _():
                step(i, j, None)

            @pl.when(jnp.logical_not(whole))
            def _():
                step(i, j, near * TILE)

            return inner

        lax.fori_loop(start, stop, key_tile, 0)
        return carry

    lax.fori_loop(0, q_tiles, query_tile, 0)


def forward_kernel(low_ref, first_ref, last_ref, q_ref, k_ref, v_ref, col_ref, row_ref, *rest, block_off, query_off, scale):
    out_ref = rest[-1]
    if len(rest) == 2:
        out_ref[...] = rest[0][...]
    else:
        out_ref[...] = jnp.zeros(out_ref.shape, f32)

    def step(i, j, reach):
        rows, cols = aligned(i * TILE, TILE), aligned(j * TILE, TILE)
        half = dot(q_ref[rows, :], k_ref[cols, :], NT) * (0.5 * scale)
        if reach is not None:
            pos_q = lax.broadcasted_iota(jnp.int32, (TILE, TILE), 0)
            pos_k = lax.broadcasted_iota(jnp.int32, (TILE, TILE), 1)
            id_q = col_ref[aligned((query_off + i) * TILE, TILE), :]
            id_k = row_ref[:, aligned((block_off + j) * TILE, TILE)]
            half = jnp.where((id_q == id_k) & (pos_k - pos_q <= reach), half, 0.0)
        weights = half + half * jnp.tanh(half)
        out_ref[rows, :] += dot(weights.astype(bf16), v_ref[cols, :])

    for_tiles(
        low_ref, first_ref, last_ref, q_ref.shape[0] // TILE, k_ref.shape[0] // TILE, block_off, query_off, step
    )


def backward_kernel(low_ref, first_ref, last_ref, core_ref, q_ref, g_ref, k_ref, v_ref, col_ref, row_ref, w_ref, slope_ref, *rest, block_off, query_off, scale):
    own = block_off == query_off
    *before, send_ref, keep_ref, grads_ref, dq_ref, dk_ref, dv_ref = rest
    width = k_ref.shape[1]
    if before:
        dq_ref[...] = before[0][...]
    else:
        dq_ref[...] = jnp.zeros(dq_ref.shape, f32)
    dk_ref[...] = jnp.zeros(dk_ref.shape, f32)
    dv_ref[...] = jnp.zeros(dv_ref.shape, f32)

    def step(i, j, reach):
        rows, cols = aligned(i * TILE, TILE), aligned(j * TILE, TILE)
        q = q_ref[rows, :]
        g = g_ref[rows, :]
        k = k_ref[cols, :]
        half = dot(k, q, NT) * (0.5 * scale)
        grad = dot(v_ref[cols, :], g, NT)
        if reach is not None:
            pos_k = lax.broadcasted_iota(jnp.int32, (TILE, TILE), 0)
            pos_q = lax.broadcasted_iota(jnp.int32, (TILE, TILE), 1)
            id_k = col_ref[aligned((block_off + j) * TILE, TILE), :]
            id_q = row_ref[:, aligned((query_off + i) * TILE, TILE)]
            ok = (id_k == id_q) & (pos_k - pos_q <= reach)
            half = jnp.where(ok, half, 0.0)
            grad = jnp.where(ok, grad, 0.0)
        twice = (1.0 + jnp.tanh(half)).astype(bf16)
        weights = half.astype(bf16) * twice
        gate = twice * bf16(0.5)
        grad = (gate + weights * (bf16(1.0) - gate)) * grad.astype(bf16)
        dv_ref[cols, :] += dot(weights, g)
        dk_ref[cols, :] += dot(grad, q)
        dq_ref[rows, :] += dot(grad, k, TN)

    q_tiles = q_ref.shape[0] // TILE
    k_tiles = k_ref.shape[0] // TILE
    for_tiles(low_ref, first_ref, last_ref, q_tiles, k_tiles, block_off, query_off, step)

    def narrow(grads, part):
        into = slice(part * width, (part + 1) * width)
        grads_ref[:, into] = (grads * slope_ref[:, into].astype(f32)).astype(bf16)

    if own:
        grads_ref[:, :width] = before[1][...]
        narrow(dv_ref[...], 1)
        narrow(dq_ref[...] * scale, 2)
        narrow(dk_ref[...] * scale, 3)
    else:
        narrow(dv_ref[...], 0)
        narrow(dk_ref[...] * scale, 1)
    core = core_ref[0]
    count = send_ref.shape[0]
    send_ref[...] = dot(grads_ref[aligned((1 - core) * count, count), :], w_ref[...], NT).astype(bf16)
    keep_ref[...] = dot(grads_ref[aligned(core * count, count), :], w_ref[...], NT).astype(bf16)


def weight_kernel(normed_ref, grads_ref, *rest):
    *before, out_ref = rest
    grads = dot(normed_ref[...], grads_ref[...], TN)
    out_ref[...] = grads + before[0][...] if before else grads


def weight_own_kernel(high_ref, normed_ref, grads_ref, early_ref, kv_ref, send_ref, keep_ref, sum_ref):
    width = kv_ref.shape[1] // 2
    size = send_ref.shape[0]
    sum_ref[:, width : 4 * width] = dot(normed_ref[...], grads_ref[:, width:], TN)
    sum_ref[:, width : 2 * width] += kv_ref[:, :width]
    sum_ref[:, 3 * width : 4 * width] += kv_ref[:, width:]
    sum_ref[:, :width] = early_ref[:, :width]
    sum_ref[:, 4 * width :] = early_ref[:, width:]
    high = high_ref[0]
    send_ref[...] = sum_ref[aligned((1 - high) * size, size), :].astype(bf16)
    keep_ref[...] = sum_ref[aligned(high * size, size), :]


def assemble_kernel(place_ref, mine_ref, other_ref, in_ref, out_ref, *, scale):
    core, flip = place_ref[0], place_ref[1]
    width = out_ref.shape[1]
    half = mine_ref.shape[0] // 2
    for ref, head in ((mine_ref, core), (other_ref, 1 - core)):
        for part in range(2):
            where = (part + flip) % 2
            rows = slice(part * half, (part + 1) * half)
            for p in range(4):
                piece = ref[rows, p * width : (p + 1) * width].astype(f32) * scale
                in_ref[pl.ds(where * (half * 8) + 2 * p + head, half, stride=8), :] = piece
            piece = ref[rows, 4 * width :].astype(f32) * scale
            out_ref[head, :, aligned(where * half, half)] = piece.T


def vmem_call(kernel, tables, arrays, outs, aliases=None, scratch=(), **static):
    whole = pl.BlockSpec(memory_space=pltpu.VMEM)
    table = pl.BlockSpec(memory_space=pltpu.SMEM)
    return pl.pallas_call(
        lambda *refs: kernel(*refs, **static),
        out_shape=outs,
        in_specs=[table] * len(tables) + [whole] * len(arrays),
        out_specs=jax.tree.map(lambda _: whole, outs),
        input_output_aliases=aliases or {},
        scratch_shapes=list(scratch),
        compiler_params=pltpu.CompilerParams(vmem_limit_bytes=16 << 20),
    )(*tables, *arrays)


def layer(tokens, cotangent, weight_in, weight_out, history_ids):
    row_count, half_width = tokens.shape
    seq_count = lax.axis_size("seq")
    device_pos = lax.axis_index("seq")
    core = device_pos % 2
    pair = device_pos // 2
    odd = pair % 2 == 1
    block = 2 * row_count
    width = 2 * half_width
    head_size = weight_out.shape[1]
    scale = head_size ** (-0.5)
    if (MAXLEN - 2 + block) // block != 2:
        raise ValueError("reach")
    tiles = block // TILE
    core_table = core.astype(jnp.int32).reshape(1)

    def over(array, axis, bit):
        return swap(array, axis, bit)

    far = shift(tokens, "seq", 4)
    own_other = over(tokens, "col", 1)
    own_set = (tokens, own_other, over(tokens, "seq", 1), over(own_other, "seq", 1))
    near = over(jnp.where(odd, far, tokens), "seq", 2)
    far_other = over(far, "col", 1)
    far_set = (far, far_other, over(far, "seq", 1), over(far_other, "seq", 1))
    near_other = over(near, "col", 1)
    near_set = (near, near_other, over(near, "seq", 1), over(near_other, "seq", 1))
    cot_other = over(cotangent, "col", 1)
    cot_set = (cotangent, cot_other, over(cotangent, "seq", 1), over(cot_other, "seq", 1))

    flip = lax.axis_index("col") == 1
    w_in = lax.dynamic_index_in_dim(weight_in, core, 2, keepdims=False).reshape(width, 4 * head_size)
    w_in = jnp.where(flip, jnp.roll(w_in, half_width, axis=0), w_in)
    w_out = lax.dynamic_index_in_dim(weight_out, core, 0, keepdims=False)
    w_out = jnp.where(flip, jnp.roll(w_out, half_width, axis=1), w_out)
    w_kv = jnp.concatenate([w_in[:, head_size : 2 * head_size], w_in[:, 3 * head_size :]], axis=1)

    padded = jnp.concatenate([jnp.full((2 * block,), -1, jnp.int32), history_ids])
    ids = lax.dynamic_slice_in_dim(padded, pair * block, 3 * block)
    by_tile = ids.reshape(-1, TILE)
    first, last = by_tile[:, 0], by_tile[:, -1]
    low = jnp.sum((last[None, :] < first[2 * tiles :, None]).astype(jnp.int32), axis=1)
    tables = (low, first, last)
    id_col, id_row = ids[:, None], ids[None, :]

    def shape(rows, cols, dtype=bf16):
        return jax.ShapeDtypeStruct((rows, cols), dtype)

    def project(token_set, weights):
        count = weights.shape[1] // head_size
        outs = (shape(block, width), shape(block, count * head_size)) + (shape(block, head_size),) * count
        return vmem_call(project_kernel, (core_table,), (*token_set, weights), outs)

    normed_own, slope_own, up_part, value_own, query, key_own = project(own_set, w_in)
    normed_far, slope_far, value_far, key_far = project(far_set, w_kv)
    normed_near, slope_near, value_near, key_near = project(near_set, w_kv)
    keys = [key_far, key_near, key_own]
    values = [value_far, value_near, value_own]

    def forward(which, before):
        arrays = [query, keys[which], values[which], id_col, id_row]
        aliases = {}
        if before is not None:
            aliases = {3 + len(arrays): 0}
            arrays.append(before)
        return vmem_call(
            forward_kernel,
            tables,
            arrays,
            shape(block, head_size, f32),
            aliases,
            block_off=which * tiles,
            query_off=2 * tiles,
            scale=scale,
        )

    attended = forward(2, None)
    attended = forward(0, attended)
    attended = forward(1, attended)

    grad_narrow, gated, pre_up = vmem_call(
        middle_kernel,
        (core_table,),
        (attended, up_part, slope_own, *cot_set, w_out),
        (shape(block, head_size),) * 3,
    )
    out_send, out_keep, grad_early = vmem_call(
        outer_kernel,
        (core_table,),
        (gated, pre_up, normed_own, *cot_set, w_out),
        (shape(row_count, width), shape(row_count, width), shape(width, 2 * head_size, f32)),
    )

    def over_heads(send, keep):
        keep = keep.astype(f32) + over(send, "seq", 1).astype(f32)
        return keep[:, :half_width] + over(keep[:, half_width:].astype(bf16), "col", 1).astype(f32)

    def backward(which, weights, slope, before):
        arrays = [query, grad_narrow, keys[which], values[which], id_col, id_row, weights, slope, *before]
        outs = (
            shape(row_count, width),
            shape(row_count, width),
            shape(block, weights.shape[1]),
            shape(block, head_size, f32),
        )
        return vmem_call(
            backward_kernel,
            (*tables, core_table),
            arrays,
            outs,
            {4 + 8: 3} if before else None,
            scratch=[pltpu.VMEM((block, head_size), f32)] * 2,
            block_off=which * tiles,
            query_off=2 * tiles,
            scale=scale,
        )

    kv_shape = shape(width, 2 * head_size, f32)
    near_send, near_keep, near_grads, grad_query = backward(1, w_kv, slope_near, ())
    grad_kv = vmem_call(weight_kernel, (), (normed_near, near_grads), kv_shape)
    near_part = over_heads(near_send, near_keep)
    near_back = over(near_part.astype(bf16), "seq", 2).astype(f32)
    far_send, far_keep, far_grads, grad_query = backward(0, w_kv, slope_far, (grad_query,))
    grad_kv = vmem_call(weight_kernel, (), (normed_far, far_grads, grad_kv), kv_shape)
    far_part = over_heads(far_send, far_keep) + jnp.where(odd, near_back, 0.0)
    far_back = shift(far_part.astype(bf16), "seq", -4).astype(f32)
    own_send, own_keep, own_grads, _ = backward(2, w_in, slope_own, (grad_query, pre_up))
    own_part = over_heads(own_send, own_keep)
    grad_normed = own_part + jnp.where(odd, 0.0, near_back) + far_back
    out = (tokens.astype(f32) + over_heads(out_send, out_keep)).astype(bf16)

    bits = []
    while 2 << len(bits) < seq_count:
        bits.append(2 << len(bits))
    high = ((device_pos // bits[0]) % 2).astype(jnp.int32).reshape(1)
    half_shape = (half_width, 5 * head_size)
    sent, total = vmem_call(
        weight_own_kernel,
        (high,),
        (normed_own, own_grads, grad_early, grad_kv),
        (shape(*half_shape), shape(*half_shape, f32)),
        scratch=[pltpu.VMEM((width, 5 * head_size), f32)],
    )
    for bit in bits:
        if bit != bits[0]:
            size = total.shape[0] // 2
            side = (device_pos & bit) // bit
            sent = lax.dynamic_slice_in_dim(total, (1 - side) * size, size).astype(bf16)
            total = lax.dynamic_slice_in_dim(total, side * size, size)
        total = total + over(sent, "seq", bit).astype(f32)
    total = total.astype(bf16)
    for bit in reversed(bits):
        other = over(total, "seq", bit)
        total = jnp.where(
            (device_pos & bit) != 0,
            jnp.concatenate([other, total], axis=0),
            jnp.concatenate([total, other], axis=0),
        )

    place = jnp.stack([core, lax.axis_index("col")]).astype(jnp.int32)
    grad_weight_in, grad_weight_out = vmem_call(
        assemble_kernel,
        (place,),
        (total, over(total, "seq", 1)),
        (shape(8 * width, head_size, f32), jax.ShapeDtypeStruct((2, head_size, width), f32)),
        scale=1.0 / math.sqrt(row_count * seq_count),
    )
    grad_weight_in = grad_weight_in.reshape(width, 4, 2, head_size)

    own_wide = jnp.concatenate([tokens, own_other], axis=1).astype(f32)
    normed, inv_std = layer_norm(own_wide, epsilon)
    normed = normed[:, :half_width]
    sums = jnp.stack([jnp.sum(grad_normed, axis=1), jnp.sum(grad_normed * normed, axis=1)])
    sums = (sums + over(sums, "col", 1)) / width
    grad_tokens = inv_std * (grad_normed - sums[0][:, None] - normed * sums[1][:, None])
    grad_tokens = (grad_tokens + cotangent.astype(f32)).astype(bf16)
    return (out, grad_tokens, grad_weight_in, grad_weight_out)


def solution(mesh):
    placed = (
        P("seq", "col"),
        P("seq", "col"),
        P(None, None, "col", None),
        P("col", None, None),
        P(),
    )
    return jax.shard_map(
        layer,
        mesh=mesh,
        in_specs=placed,
        out_specs=(
            P("seq", "col"),
            P("seq", "col"),
            P(None, None, "col", None),
            P("col", None, None),
        ),
        check_vma=False,
    )
```

```python
import math

import jax
import jax.numpy as jnp
from jax import lax
from jax.experimental import pallas as pl
from jax.experimental.pallas import tpu as pltpu
from jax.sharding import PartitionSpec as P

MAXLEN = 4096
TILE = 512

epsilon = 1e-05
head_floor = 1.0
f32 = jnp.float32
bf16 = jnp.bfloat16


def swap(block, axis, bit):
    return lax.ppermute(block, axis, [(i, i ^ bit) for i in range(lax.axis_size(axis))])


def shift(block, axis, distance):
    devices = range(lax.axis_size(axis))
    return lax.ppermute(block, axis, [(i, i + distance) for i in devices if i + distance in devices])


def layer_norm(values, offset):
    center = values - jnp.mean(values, axis=-1, keepdims=True)
    inv_std = lax.rsqrt(jnp.mean(center * center, axis=-1, keepdims=True) + offset)
    return (center * inv_std, inv_std)


def norm_back(grad_in, normed, inv_std):
    return inv_std * (
        grad_in
        - jnp.mean(grad_in, axis=-1, keepdims=True)
        - normed * jnp.mean(grad_in * normed, axis=-1, keepdims=True)
    )


NT = (((1,), (1,)), ((), ()))
TN = (((0,), (0,)), ((), ()))


def dot(a, b, dims=(((1,), (0,)), ((), ()))):
    return lax.dot_general(a, b, dims, preferred_element_type=f32)


def gate_of(inputs):
    return 0.5 + 0.5 * jnp.tanh(0.5 * inputs)


def aligned(start, size):
    return pl.ds(pl.multiple_of(start, size), size)


def project_kernel(core_ref, mine_a, mine_b, other_a, other_b, w_ref, normed_ref, slope_ref, *part_refs):
    size = 256
    count = mine_a.shape[0]
    core = core_ref[0]
    for first, second, where in ((mine_a, mine_b, core), (other_a, other_b, 1 - core)):

        def rows_step(step, carry, first=first, second=second, where=where):
            rows = aligned(step * size, size)
            into = aligned(where * count + step * size, size)
            values = jnp.concatenate([first[rows, :].astype(f32), second[rows, :].astype(f32)], axis=1)
            normed = layer_norm(values, epsilon)[0].astype(bf16)
            normed_ref[into, :] = normed
            pre = dot(normed, w_ref[...])
            gate = gate_of(pre)
            act = (pre * gate).astype(bf16)
            gate = gate.astype(bf16)
            slope_ref[into, :] = gate + act * (bf16(1.0) - gate)
            width = part_refs[0].shape[1]
            for p, part in enumerate(part_refs):
                part[into, :] = act[:, p * width : (p + 1) * width]
            return carry

        lax.fori_loop(0, count // size, rows_step, 0)


def middle_kernel(core_ref, att_ref, up_ref, slope_ref, mine_a, mine_b, other_a, other_b, w_ref, narrow_ref, gated_ref, pre_up_ref):
    size = 256
    count = mine_a.shape[0]
    half = mine_a.shape[1]
    core = core_ref[0]
    for first, second, where in ((mine_a, mine_b, core), (other_a, other_b, 1 - core)):

        def rows_step(step, carry, first=first, second=second, where=where):
            rows = aligned(step * size, size)
            into = aligned(where * count + step * size, size)
            head_normed, head_scale = layer_norm(att_ref[into, :], head_floor)
            up = up_ref[into, :].astype(f32)
            gated_ref[into, :] = (head_normed * up).astype(bf16)
            grad = dot(first[rows, :], w_ref[:, :half], NT) + dot(second[rows, :], w_ref[:, half:], NT)
            pre_up_ref[into, :] = (grad * head_normed * slope_ref[into, : up.shape[1]].astype(f32)).astype(bf16)
            narrow_ref[into, :] = norm_back(grad * up, head_normed, head_scale).astype(bf16)
            return carry

        lax.fori_loop(0, count // size, rows_step, 0)


def outer_kernel(core_ref, gated_ref, pre_up_ref, normed_ref, mine_a, mine_b, other_a, other_b, w_ref, send_ref, keep_ref, grad_ref):
    count, half = mine_a.shape
    width = gated_ref.shape[1]
    core = core_ref[0]
    mine = aligned(core * count, count)
    other = aligned((1 - core) * count, count)
    send_ref[...] = dot(gated_ref[other, :], w_ref[...]).astype(bf16)
    keep_ref[...] = dot(gated_ref[mine, :], w_ref[...]).astype(bf16)
    grad_ref[:, :width] = dot(normed_ref[...], pre_up_ref[...], TN)
    grad_ref[:half, width:] = dot(mine_a[...], gated_ref[mine, :], TN) + dot(other_a[...], gated_ref[other, :], TN)
    grad_ref[half:, width:] = dot(mine_b[...], gated_ref[mine, :], TN) + dot(other_b[...], gated_ref[other, :], TN)


def for_tiles(low_ref, first_ref, last_ref, q_tiles, k_tiles, block_off, query_off, step):
    def query_tile(i, carry):
        start = jnp.maximum(low_ref[i] - block_off, 0)
        stop = jnp.minimum(query_off + i + 1 - block_off, k_tiles)

        def key_tile(j, inner):
            near = query_off + i - block_off - j
            whole = (near > 0) & (first_ref[block_off + j] == last_ref[query_off + i])

            @pl.when(whole)
            def _():
                step(i, j, None)

            @pl.when(jnp.logical_not(whole))
            def _():
                step(i, j, near * TILE)

            return inner

        lax.fori_loop(start, stop, key_tile, 0)
        return carry

    lax.fori_loop(0, q_tiles, query_tile, 0)


def forward_kernel(low_ref, first_ref, last_ref, q_ref, k_ref, v_ref, col_ref, row_ref, *rest, block_off, query_off, scale):
    out_ref = rest[-1]
    if len(rest) == 2:
        out_ref[...] = rest[0][...]
    else:
        out_ref[...] = jnp.zeros(out_ref.shape, f32)

    def step(i, j, reach):
        rows, cols = aligned(i * TILE, TILE), aligned(j * TILE, TILE)
        half = dot(q_ref[rows, :], k_ref[cols, :], NT) * (0.5 * scale)
        if reach is not None:
            pos_q = lax.broadcasted_iota(jnp.int32, (TILE, TILE), 0)
            pos_k = lax.broadcasted_iota(jnp.int32, (TILE, TILE), 1)
            id_q = col_ref[aligned((query_off + i) * TILE, TILE), :]
            id_k = row_ref[:, aligned((block_off + j) * TILE, TILE)]
            half = jnp.where((id_q == id_k) & (pos_k - pos_q <= reach), half, 0.0)
        weights = half + half * jnp.tanh(half)
        out_ref[rows, :] += dot(weights.astype(bf16), v_ref[cols, :])

    for_tiles(
        low_ref, first_ref, last_ref, q_ref.shape[0] // TILE, k_ref.shape[0] // TILE, block_off, query_off, step
    )


def backward_kernel(low_ref, first_ref, last_ref, core_ref, q_ref, g_ref, k_ref, v_ref, col_ref, row_ref, w_ref, slope_ref, *rest, block_off, query_off, scale):
    own = block_off == query_off
    *before, send_ref, keep_ref, grads_ref, dq_ref, dk_ref, dv_ref = rest
    width = k_ref.shape[1]
    if before:
        dq_ref[...] = before[0][...]
    else:
        dq_ref[...] = jnp.zeros(dq_ref.shape, f32)
    dk_ref[...] = jnp.zeros(dk_ref.shape, f32)
    dv_ref[...] = jnp.zeros(dv_ref.shape, f32)

    def step(i, j, reach):
        rows, cols = aligned(i * TILE, TILE), aligned(j * TILE, TILE)
        q = q_ref[rows, :]
        g = g_ref[rows, :]
        k = k_ref[cols, :]
        half = dot(k, q, NT) * (0.5 * scale)
        grad = dot(v_ref[cols, :], g, NT)
        if reach is not None:
            pos_k = lax.broadcasted_iota(jnp.int32, (TILE, TILE), 0)
            pos_q = lax.broadcasted_iota(jnp.int32, (TILE, TILE), 1)
            id_k = col_ref[aligned((block_off + j) * TILE, TILE), :]
            id_q = row_ref[:, aligned((query_off + i) * TILE, TILE)]
            ok = (id_k == id_q) & (pos_k - pos_q <= reach)
            half = jnp.where(ok, half, 0.0)
            grad = jnp.where(ok, grad, 0.0)
        twice = (1.0 + jnp.tanh(half)).astype(bf16)
        weights = half.astype(bf16) * twice
        gate = twice * bf16(0.5)
        grad = (gate + weights * (bf16(1.0) - gate)) * grad.astype(bf16)
        dv_ref[cols, :] += dot(weights, g)
        dk_ref[cols, :] += dot(grad, q)
        dq_ref[rows, :] += dot(grad, k, TN)

    q_tiles = q_ref.shape[0] // TILE
    k_tiles = k_ref.shape[0] // TILE
    for_tiles(low_ref, first_ref, last_ref, q_tiles, k_tiles, block_off, query_off, step)

    if own:
        grads_ref[:, :width] = before[1][...]
    parts = ((1, dv_ref), (2, dq_ref), (3, dk_ref)) if own else ((0, dv_ref), (1, dk_ref))

    def narrow(step, carry):
        rows = aligned(step * 256, 256)
        for part, ref in parts:
            into = slice(part * width, (part + 1) * width)
            grads = ref[rows, :] if ref is dv_ref else ref[rows, :] * scale
            grads_ref[rows, into] = (grads * slope_ref[rows, into].astype(f32)).astype(bf16)
        return carry

    lax.fori_loop(0, dk_ref.shape[0] // 256, narrow, 0)
    core = core_ref[0]
    count = send_ref.shape[0]
    send_ref[...] = dot(grads_ref[aligned((1 - core) * count, count), :], w_ref[...], NT).astype(bf16)
    keep_ref[...] = dot(grads_ref[aligned(core * count, count), :], w_ref[...], NT).astype(bf16)


def weight_kernel(normed_ref, grads_ref, *rest):
    grads = dot(normed_ref[...], grads_ref[...], TN)
    rest[-1][...] = grads if len(rest) == 1 else grads + rest[0][...]


def weight_own_kernel(side_ref, normed_ref, grads_ref, early_ref, kv_ref, send_ref, keep_ref, sum_ref):
    width = kv_ref.shape[1] // 2
    sum_ref[:, width : 4 * width] = dot(normed_ref[...], grads_ref[:, width:], TN)
    sum_ref[:, width : 2 * width] += kv_ref[:, :width]
    sum_ref[:, 3 * width : 4 * width] += kv_ref[:, width:]
    sum_ref[:, :width] = early_ref[:, :width]
    sum_ref[:, 4 * width :] = early_ref[:, width:]
    side = side_ref[0]
    size = send_ref.shape[0]
    send_ref[...] = sum_ref[aligned((1 - side) * size, size), :].astype(bf16)
    keep_ref[...] = sum_ref[aligned(side * size, size), :]


def last_kernel(kept_ref, received_ref, out_ref):
    out_ref[...] = (kept_ref[...] + received_ref[...].astype(f32)).astype(bf16)


def halve_kernel(side_ref, kept_ref, received_ref, send_ref, keep_ref):
    side = side_ref[0]
    size = send_ref.shape[0]
    other, mine = aligned((1 - side) * size, size), aligned(side * size, size)
    send_ref[...] = (kept_ref[other, :] + received_ref[other, :].astype(f32)).astype(bf16)
    keep_ref[...] = kept_ref[mine, :] + received_ref[mine, :].astype(f32)


def assemble_kernel(place_ref, mine_ref, other_ref, in_ref, out_ref, turned_ref, *, scale, blocks):
    core, place = place_ref[0], place_ref[1]
    width = turned_ref.shape[1]
    size = mine_ref.shape[0] // blocks
    for ref, head in ((mine_ref, core), (other_ref, 1 - core)):
        for i in range(blocks):
            rows = slice(i * size, (i + 1) * size)
            true = jnp.bitwise_xor(i, place) * size
            for p in range(4):
                piece = ref[rows, p * width : (p + 1) * width].astype(f32) * scale
                in_ref[pl.ds(true * 8 + 2 * p + head, size, stride=8), :] = piece
            turned_ref[aligned(true, size), :] = ref[rows, 4 * width :].astype(f32) * scale
        out_ref[head] = turned_ref[...].T


def vmem_call(kernel, tables, arrays, outs, aliases=None, scratch=(), **static):
    whole = pl.BlockSpec(memory_space=pltpu.VMEM)
    table = pl.BlockSpec(memory_space=pltpu.SMEM)
    return pl.pallas_call(
        lambda *refs: kernel(*refs, **static),
        out_shape=outs,
        in_specs=[table] * len(tables) + [whole] * len(arrays),
        out_specs=jax.tree.map(lambda _: whole, outs),
        input_output_aliases=aliases or {},
        scratch_shapes=list(scratch),
        compiler_params=pltpu.CompilerParams(vmem_limit_bytes=16 << 20),
    )(*tables, *arrays)


def layer(tokens, cotangent, weight_in, weight_out, history_ids):
    row_count, half_width = tokens.shape
    seq_count = lax.axis_size("seq")
    device_pos = lax.axis_index("seq")
    core = device_pos % 2
    pair = device_pos // 2
    odd = pair % 2 == 1
    block = 2 * row_count
    width = 2 * half_width
    head_size = weight_out.shape[1]
    scale = head_size ** (-0.5)
    if (MAXLEN - 2 + block) // block != 2:
        raise ValueError("reach")
    tiles = block // TILE
    core_table = core.astype(jnp.int32).reshape(1)

    def over(array, axis, bit):
        return swap(array, axis, bit)

    flip = lax.axis_index("col") == 1
    w_in = lax.dynamic_index_in_dim(weight_in, core, 2, keepdims=False).reshape(width, 4 * head_size)
    w_in = jnp.where(flip, jnp.roll(w_in, half_width, axis=0), w_in)
    w_out = lax.dynamic_index_in_dim(weight_out, core, 0, keepdims=False)
    w_out = jnp.where(flip, jnp.roll(w_out, half_width, axis=1), w_out)
    w_kv = jnp.concatenate([w_in[:, head_size : 2 * head_size], w_in[:, 3 * head_size :]], axis=1)

    padded = jnp.concatenate([jnp.full((2 * block,), -1, jnp.int32), history_ids])
    ids = lax.dynamic_slice_in_dim(padded, pair * block, 3 * block)
    by_tile = ids.reshape(-1, TILE)
    first, last = by_tile[:, 0], by_tile[:, -1]
    low = jnp.sum((last[None, :] < first[2 * tiles :, None]).astype(jnp.int32), axis=1)
    tables = (low, first, last)
    id_col, id_row = ids[:, None], ids[None, :]

    far = shift(tokens, "seq", 4)
    own_other = over(tokens, "col", 1)
    own_other, w_in, w_kv, w_out, id_col, id_row, tables = lax.optimization_barrier(
        (own_other, w_in, w_kv, w_out, id_col, id_row, tables)
    )
    own_set = (tokens, own_other, over(tokens, "seq", 1), over(own_other, "seq", 1))

    def shape(rows, cols, dtype=bf16):
        return jax.ShapeDtypeStruct((rows, cols), dtype)

    def project(token_set, weights):
        count = weights.shape[1] // head_size
        outs = (shape(block, width), shape(block, count * head_size)) + (shape(block, head_size),) * count
        return vmem_call(project_kernel, (core_table,), (*token_set, weights), outs)

    normed_own, slope_own, up_part, value_own, query, key_own = project(own_set, w_in)
    near = over(jnp.where(odd, far, tokens), "seq", 2)
    far_other = over(far, "col", 1)
    far_set = (far, far_other, over(lax.optimization_barrier((far, query))[0], "seq", 1), over(far_other, "seq", 1))
    near_other = over(near, "col", 1)
    near_set = (near, near_other, over(near, "seq", 1), over(near_other, "seq", 1))
    cot_other = over(cotangent, "col", 1)
    cot_set = (cotangent, cot_other, over(cotangent, "seq", 1), over(cot_other, "seq", 1))

    normed_far, slope_far, value_far, key_far = project(far_set, w_kv)
    normed_near, slope_near, value_near, key_near = project(near_set, w_kv)
    keys = [key_far, key_near, key_own]
    values = [value_far, value_near, value_own]

    def forward(which, before):
        arrays = [query, keys[which], values[which], id_col, id_row]
        aliases = {}
        if before is not None:
            aliases = {3 + len(arrays): 0}
            arrays.append(before)
        return vmem_call(
            forward_kernel,
            tables,
            arrays,
            shape(block, head_size, f32),
            aliases,
            block_off=which * tiles,
            query_off=2 * tiles,
            scale=scale,
        )

    attended = forward(2, None)
    attended = forward(0, attended)
    attended = forward(1, attended)

    grad_narrow, gated, pre_up = vmem_call(
        middle_kernel,
        (core_table,),
        (attended, up_part, slope_own, *cot_set, w_out),
        (shape(block, head_size),) * 3,
    )
    out_send, out_keep, grad_early = vmem_call(
        outer_kernel,
        (core_table,),
        (gated, pre_up, normed_own, *cot_set, w_out),
        (shape(row_count, width), shape(row_count, width), shape(width, 2 * head_size, f32)),
    )

    def over_heads(send, keep):
        keep = keep.astype(f32) + over(send, "seq", 1).astype(f32)
        return keep[:, :half_width] + over(keep[:, half_width:].astype(bf16), "col", 1).astype(f32)

    def backward(which, weights, slope, before):
        arrays = [query, grad_narrow, keys[which], values[which], id_col, id_row, weights, slope, *before]
        outs = (
            shape(row_count, width),
            shape(row_count, width),
            shape(block, weights.shape[1]),
            shape(block, head_size, f32),
        )
        return vmem_call(
            backward_kernel,
            (*tables, core_table),
            arrays,
            outs,
            {4 + 8: 3} if before else None,
            scratch=[pltpu.VMEM((block, head_size), f32)] * 2,
            block_off=which * tiles,
            query_off=2 * tiles,
            scale=scale,
        )

    kv_shape = shape(width, 2 * head_size, f32)
    near_send, near_keep, near_grads, grad_query = backward(1, w_kv, slope_near, ())
    grad_kv = vmem_call(weight_kernel, (), (normed_near, near_grads), kv_shape)
    near_part = over_heads(near_send, near_keep)
    near_back = over(near_part.astype(bf16), "seq", 2).astype(f32)
    far_send, far_keep, far_grads, grad_query = backward(0, w_kv, slope_far, (grad_query,))
    grad_kv = vmem_call(weight_kernel, (), (normed_far, far_grads, grad_kv), kv_shape)
    far_part = over_heads(far_send, far_keep) + jnp.where(odd, near_back, 0.0)
    far_back = shift(far_part.astype(bf16), "seq", -4).astype(f32)
    own_send, own_keep, own_grads, _ = backward(2, w_in, slope_own, (grad_query, pre_up))
    own_part = over_heads(own_send, own_keep)
    grad_normed = own_part + jnp.where(odd, 0.0, near_back) + far_back
    out = (tokens.astype(f32) + over_heads(out_send, out_keep)).astype(bf16)

    bits = []
    while 2 << len(bits) < seq_count:
        bits.append(2 << len(bits))
    sides = [((device_pos // bit) % 2).astype(jnp.int32) for bit in bits]
    lanes = 5 * head_size
    size = half_width
    sent, kept = vmem_call(
        weight_own_kernel,
        (sides[0].reshape(1),),
        (normed_own, own_grads, grad_early, grad_kv),
        (shape(size, lanes), shape(size, lanes, f32)),
        scratch=[pltpu.VMEM((width, lanes), f32)],
    )
    for i, bit in enumerate(bits):
        received = over(sent, "seq", bit)
        if i + 1 < len(bits):
            size = size // 2
            sent, kept = vmem_call(
                halve_kernel,
                (sides[i + 1].reshape(1),),
                (kept, received),
                (shape(size, lanes), shape(size, lanes, f32)),
            )
        else:
            total = vmem_call(last_kernel, (), (kept, received), shape(size, lanes))
    for i, bit in reversed(list(enumerate(bits))):
        total = jnp.concatenate([total, over(total, "seq", bit)], axis=0)

    blocks = 1 << len(bits)
    block_place = lax.axis_index("col") * (blocks // 2)
    for i, side in enumerate(sides):
        block_place = block_place ^ (side << (len(bits) - 1 - i))
    place = jnp.stack([core, block_place]).astype(jnp.int32)
    grad_weight_in, grad_weight_out = vmem_call(
        assemble_kernel,
        (place,),
        (total, over(total, "seq", 1)),
        (shape(8 * width, head_size, f32), jax.ShapeDtypeStruct((2, head_size, width), f32)),
        scratch=[pltpu.VMEM((width, head_size), f32)],
        scale=1.0 / math.sqrt(row_count * seq_count),
        blocks=blocks,
    )
    grad_weight_in = grad_weight_in.reshape(width, 4, 2, head_size)

    own_wide = jnp.concatenate([tokens, own_other], axis=1).astype(f32)
    normed, inv_std = layer_norm(own_wide, epsilon)
    normed = normed[:, :half_width]
    sums = jnp.stack([jnp.sum(grad_normed, axis=1), jnp.sum(grad_normed * normed, axis=1)])
    sums = (sums + over(sums, "col", 1)) / width
    grad_tokens = inv_std * (grad_normed - sums[0][:, None] - normed * sums[1][:, None])
    grad_tokens = (grad_tokens + cotangent.astype(f32)).astype(bf16)
    return (out, grad_tokens, grad_weight_in, grad_weight_out)


def solution(mesh):
    placed = (
        P("seq", "col"),
        P("seq", "col"),
        P(None, None, "col", None),
        P("col", None, None),
        P(),
    )
    return jax.shard_map(
        layer,
        mesh=mesh,
        in_specs=placed,
        out_specs=(
            P("seq", "col"),
            P("seq", "col"),
            P(None, None, "col", None),
            P("col", None, None),
        ),
        check_vma=False,
    )
```

```python
import math

import jax
import jax.numpy as jnp
from jax import lax
from jax.experimental import pallas as pl
from jax.experimental.pallas import tpu as pltpu
from jax.sharding import PartitionSpec as P

MAXLEN = 4096
TILE = 512

epsilon = 1e-05
head_floor = 1.0
f32 = jnp.float32
bf16 = jnp.bfloat16


def swap(block, axis, bit):
    return lax.ppermute(block, axis, [(i, i ^ bit) for i in range(lax.axis_size(axis))])


def shift(block, axis, distance):
    devices = range(lax.axis_size(axis))
    return lax.ppermute(block, axis, [(i, i + distance) for i in devices if i + distance in devices])


def layer_norm(values, offset):
    center = values - jnp.mean(values, axis=-1, keepdims=True)
    inv_std = lax.rsqrt(jnp.mean(center * center, axis=-1, keepdims=True) + offset)
    return (center * inv_std, inv_std)


def norm_back(grad_in, normed, inv_std):
    return inv_std * (
        grad_in
        - jnp.mean(grad_in, axis=-1, keepdims=True)
        - normed * jnp.mean(grad_in * normed, axis=-1, keepdims=True)
    )


NT = (((1,), (1,)), ((), ()))
TN = (((0,), (0,)), ((), ()))


def dot(a, b, dims=(((1,), (0,)), ((), ()))):
    return lax.dot_general(a, b, dims, preferred_element_type=f32)


def gate_of(inputs):
    return 0.5 + 0.5 * jnp.tanh(0.5 * inputs)


def column_of(row):
    count = row.shape[1]
    turned = jnp.broadcast_to(row, (128, count)).T
    return jnp.concatenate([turned] * (count // 128), axis=1)


def aligned(start, size):
    return pl.ds(pl.multiple_of(start, size), size)


def project_kernel(core_ref, mine_a, mine_b, other_a, other_b, w_ref, normed_ref, slope_ref, *part_refs):
    size = 256
    count = mine_a.shape[0]
    core = core_ref[0]
    for first, second, where in ((mine_a, mine_b, core), (other_a, other_b, 1 - core)):

        def rows_step(step, carry, first=first, second=second, where=where):
            rows = aligned(step * size, size)
            into = aligned(where * count + step * size, size)
            values = jnp.concatenate([first[rows, :].astype(f32), second[rows, :].astype(f32)], axis=1)
            normed = layer_norm(values, epsilon)[0].astype(bf16)
            normed_ref[into, :] = normed
            pre = dot(normed, w_ref[...])
            gate = gate_of(pre)
            act = (pre * gate).astype(bf16)
            gate = gate.astype(bf16)
            slope_ref[into, :] = gate + act * (bf16(1.0) - gate)
            width = part_refs[0].shape[1]
            for p, part in enumerate(part_refs):
                part[into, :] = act[:, p * width : (p + 1) * width]
            return carry

        lax.fori_loop(0, count // size, rows_step, 0)


def middle_kernel(core_ref, att_ref, up_ref, slope_ref, mine_a, mine_b, other_a, other_b, w_ref, narrow_ref, gated_ref, pre_up_ref):
    size = 256
    count = mine_a.shape[0]
    half = mine_a.shape[1]
    core = core_ref[0]
    for first, second, where in ((mine_a, mine_b, core), (other_a, other_b, 1 - core)):

        def rows_step(step, carry, first=first, second=second, where=where):
            rows = aligned(step * size, size)
            into = aligned(where * count + step * size, size)
            head_normed, head_scale = layer_norm(att_ref[into, :], head_floor)
            up = up_ref[into, :].astype(f32)
            gated_ref[into, :] = (head_normed * up).astype(bf16)
            grad = dot(first[rows, :], w_ref[:, :half], NT) + dot(second[rows, :], w_ref[:, half:], NT)
            pre_up_ref[into, :] = (grad * head_normed * slope_ref[into, : up.shape[1]].astype(f32)).astype(bf16)
            narrow_ref[into, :] = norm_back(grad * up, head_normed, head_scale).astype(bf16)
            return carry

        lax.fori_loop(0, count // size, rows_step, 0)


def outer_kernel(core_ref, gated_ref, pre_up_ref, normed_ref, mine_a, mine_b, other_a, other_b, w_ref, send_ref, keep_ref, grad_ref):
    count, half = mine_a.shape
    width = gated_ref.shape[1]
    core = core_ref[0]
    mine = aligned(core * count, count)
    other = aligned((1 - core) * count, count)
    send_ref[...] = dot(gated_ref[other, :], w_ref[...]).astype(bf16)
    keep_ref[...] = dot(gated_ref[mine, :], w_ref[...]).astype(bf16)
    grad_ref[:, :width] = dot(normed_ref[...], pre_up_ref[...], TN)
    grad_ref[:half, width:] = dot(mine_a[...], gated_ref[mine, :], TN) + dot(other_a[...], gated_ref[other, :], TN)
    grad_ref[half:, width:] = dot(mine_b[...], gated_ref[mine, :], TN) + dot(other_b[...], gated_ref[other, :], TN)


def for_tiles(low_ref, first_ref, last_ref, q_tiles, k_tiles, block_off, query_off, step):
    def query_tile(i, carry):
        start = jnp.maximum(low_ref[i] - block_off, 0)
        stop = jnp.minimum(query_off + i + 1 - block_off, k_tiles)

        def key_tile(j, inner):
            near = query_off + i - block_off - j
            whole = (near > 0) & (first_ref[block_off + j] == last_ref[query_off + i])

            @pl.when(whole)
            def _():
                step(i, j, None)

            @pl.when(jnp.logical_not(whole))
            def _():
                step(i, j, near * TILE)

            return inner

        lax.fori_loop(start, stop, key_tile, 0)
        return carry

    lax.fori_loop(0, q_tiles, query_tile, 0)


def forward_kernel(low_ref, first_ref, last_ref, q_ref, k_ref, v_ref, row_ref, *rest, block_off, query_off, scale):
    out_ref = rest[-1]
    if len(rest) == 2:
        out_ref[...] = rest[0][...]
    else:
        out_ref[...] = jnp.zeros(out_ref.shape, f32)

    def step(i, j, reach):
        rows, cols = aligned(i * TILE, TILE), aligned(j * TILE, TILE)
        half = dot(q_ref[rows, :], k_ref[cols, :], NT) * (0.5 * scale)
        if reach is not None:
            pos_q = lax.broadcasted_iota(jnp.int32, (TILE, TILE), 0)
            pos_k = lax.broadcasted_iota(jnp.int32, (TILE, TILE), 1)
            id_q = column_of(row_ref[:, aligned((query_off + i) * TILE, TILE)])
            id_k = row_ref[:, aligned((block_off + j) * TILE, TILE)]
            half = jnp.where((id_q == id_k) & (pos_k - pos_q <= reach), half, 0.0)
        weights = half + half * jnp.tanh(half)
        out_ref[rows, :] += dot(weights.astype(bf16), v_ref[cols, :])

    for_tiles(
        low_ref, first_ref, last_ref, q_ref.shape[0] // TILE, k_ref.shape[0] // TILE, block_off, query_off, step
    )


def backward_kernel(low_ref, first_ref, last_ref, core_ref, q_ref, g_ref, k_ref, v_ref, row_ref, w_ref, slope_ref, *rest, block_off, query_off, scale):
    own = block_off == query_off
    *before, send_ref, keep_ref, grads_ref, dq_ref, dk_ref, dv_ref = rest
    width = k_ref.shape[1]
    if before:
        dq_ref[...] = before[0][...]
    else:
        dq_ref[...] = jnp.zeros(dq_ref.shape, f32)
    dk_ref[...] = jnp.zeros(dk_ref.shape, f32)
    dv_ref[...] = jnp.zeros(dv_ref.shape, f32)

    def step(i, j, reach):
        rows, cols = aligned(i * TILE, TILE), aligned(j * TILE, TILE)
        q = q_ref[rows, :]
        g = g_ref[rows, :]
        k = k_ref[cols, :]
        half = dot(k, q, NT) * (0.5 * scale)
        grad = dot(v_ref[cols, :], g, NT)
        if reach is not None:
            pos_k = lax.broadcasted_iota(jnp.int32, (TILE, TILE), 0)
            pos_q = lax.broadcasted_iota(jnp.int32, (TILE, TILE), 1)
            id_k = column_of(row_ref[:, aligned((block_off + j) * TILE, TILE)])
            id_q = row_ref[:, aligned((query_off + i) * TILE, TILE)]
            ok = (id_k == id_q) & (pos_k - pos_q <= reach)
            half = jnp.where(ok, half, 0.0)
            grad = jnp.where(ok, grad, 0.0)
        twice = (1.0 + jnp.tanh(half)).astype(bf16)
        weights = half.astype(bf16) * twice
        gate = twice * bf16(0.5)
        grad = (gate + weights * (bf16(1.0) - gate)) * grad.astype(bf16)
        dv_ref[cols, :] += dot(weights, g)
        dk_ref[cols, :] += dot(grad, q)
        dq_ref[rows, :] += dot(grad, k, TN)

    q_tiles = q_ref.shape[0] // TILE
    k_tiles = k_ref.shape[0] // TILE
    for_tiles(low_ref, first_ref, last_ref, q_tiles, k_tiles, block_off, query_off, step)

    if own:
        grads_ref[:, :width] = before[1][...]
    parts = ((1, dv_ref), (2, dq_ref), (3, dk_ref)) if own else ((0, dv_ref), (1, dk_ref))

    def narrow(step, carry):
        rows = aligned(step * 256, 256)
        for part, ref in parts:
            into = slice(part * width, (part + 1) * width)
            grads = ref[rows, :] if ref is dv_ref else ref[rows, :] * scale
            grads_ref[rows, into] = (grads * slope_ref[rows, into].astype(f32)).astype(bf16)
        return carry

    lax.fori_loop(0, dk_ref.shape[0] // 256, narrow, 0)
    core = core_ref[0]
    count = send_ref.shape[0]
    send_ref[...] = dot(grads_ref[aligned((1 - core) * count, count), :], w_ref[...], NT).astype(bf16)
    keep_ref[...] = dot(grads_ref[aligned(core * count, count), :], w_ref[...], NT).astype(bf16)


def weight_kernel(normed_ref, grads_ref, *rest):
    grads = dot(normed_ref[...], grads_ref[...], TN)
    rest[-1][...] = grads if len(rest) == 1 else grads + rest[0][...]


def weight_own_kernel(table_ref, normed_ref, grads_ref, early_ref, kv_ref, send_ref, keep_ref, sum_ref):
    width = kv_ref.shape[1] // 2
    sum_ref[:, width : 4 * width] = dot(normed_ref[...], grads_ref[:, width:], TN)
    sum_ref[:, width : 2 * width] += kv_ref[:, :width]
    sum_ref[:, 3 * width : 4 * width] += kv_ref[:, width:]
    sum_ref[:, :width] = early_ref[:, :width]
    sum_ref[:, 4 * width :] = early_ref[:, width:]
    side = table_ref[2]
    size = send_ref.shape[0]
    send_ref[...] = sum_ref[aligned((1 - side) * size, size), :].astype(bf16)
    keep_ref[...] = sum_ref[aligned(side * size, size), :]


def last_kernel(kept_ref, received_ref, out_ref):
    out_ref[...] = (kept_ref[...] + received_ref[...].astype(f32)).astype(bf16)


def halve_kernel(table_ref, kept_ref, received_ref, send_ref, keep_ref, *, step):
    side = table_ref[2 + step]
    size = send_ref.shape[0]
    other, mine = aligned((1 - side) * size, size), aligned(side * size, size)
    send_ref[...] = (kept_ref[other, :] + received_ref[other, :].astype(f32)).astype(bf16)
    keep_ref[...] = kept_ref[mine, :] + received_ref[mine, :].astype(f32)


def assemble_kernel(place_ref, mine_ref, other_ref, in_ref, out_ref, turned_ref, *, scale, blocks):
    core, place = place_ref[0], place_ref[1]
    width = turned_ref.shape[1]
    size = mine_ref.shape[0] // blocks
    for ref, head in ((mine_ref, core), (other_ref, 1 - core)):
        for i in range(blocks):
            rows = slice(i * size, (i + 1) * size)
            true = jnp.bitwise_xor(i, place) * size
            for p in range(4):
                piece = ref[rows, p * width : (p + 1) * width].astype(f32) * scale
                in_ref[pl.ds(true * 8 + 2 * p + head, size, stride=8), :] = piece
            turned_ref[aligned(true, size), :] = ref[rows, 4 * width :].astype(f32) * scale
        out_ref[head] = turned_ref[...].T


def vmem_call(kernel, tables, arrays, outs, aliases=None, scratch=(), **static):
    whole = pl.BlockSpec(memory_space=pltpu.VMEM)
    table = pl.BlockSpec(memory_space=pltpu.SMEM)
    return pl.pallas_call(
        lambda *refs: kernel(*refs, **static),
        out_shape=outs,
        in_specs=[table] * len(tables) + [whole] * len(arrays),
        out_specs=jax.tree.map(lambda _: whole, outs),
        input_output_aliases=aliases or {},
        scratch_shapes=list(scratch),
        compiler_params=pltpu.CompilerParams(vmem_limit_bytes=16 << 20),
    )(*tables, *arrays)


def layer(tokens, cotangent, weight_in, weight_out, history_ids):
    row_count, half_width = tokens.shape
    seq_count = lax.axis_size("seq")
    device_pos = lax.axis_index("seq")
    core = device_pos & 1
    pair = device_pos >> 1
    odd = (device_pos & 2) != 0
    block = 2 * row_count
    width = 2 * half_width
    head_size = weight_out.shape[1]
    scale = head_size ** (-0.5)
    if (MAXLEN - 2 + block) // block != 2:
        raise ValueError("reach")
    tiles = block // TILE

    bits = []
    while 2 << len(bits) < seq_count:
        bits.append(2 << len(bits))
    steps = len(bits)
    block_place = lax.axis_index("col") << (steps - 1)
    for i in range(steps):
        block_place = block_place ^ (((device_pos >> (i + 1)) & 1) << (steps - 1 - i))
    table = jnp.stack([core, block_place] + [(device_pos >> (i + 1)) & 1 for i in range(steps)]).astype(jnp.int32)

    def over(array, axis, bit):
        return swap(array, axis, bit)

    flip = lax.axis_index("col") != 0
    w_in = lax.dynamic_index_in_dim(weight_in, core, 2, keepdims=False).reshape(width, 4 * head_size)
    w_in = jnp.where(flip, jnp.roll(w_in, half_width, axis=0), w_in)
    w_out = lax.dynamic_index_in_dim(weight_out, core, 0, keepdims=False)
    w_out = jnp.where(flip, jnp.roll(w_out, half_width, axis=1), w_out)
    w_kv = jnp.concatenate([w_in[:, head_size : 2 * head_size], w_in[:, 3 * head_size :]], axis=1)

    padded = jnp.concatenate([jnp.full((2 * block,), -1, jnp.int32), history_ids])
    ids = lax.dynamic_slice_in_dim(padded, pair * block, 3 * block)
    by_tile = ids.reshape(-1, TILE)
    first, last = by_tile[:, 0], by_tile[:, -1]
    low = jnp.sum((last[None, :] < first[2 * tiles :, None]).astype(jnp.int32), axis=1)
    tables = (low, first, last)
    id_row = ids[None, :]

    far = shift(tokens, "seq", 4)
    own_other = over(tokens, "col", 1)
    own_other, w_in, w_kv, w_out, id_row, tables, table, odd = lax.optimization_barrier(
        (own_other, w_in, w_kv, w_out, id_row, tables, table, odd)
    )
    own_set = (tokens, own_other, over(tokens, "seq", 1), over(own_other, "seq", 1))

    def shape(rows, cols, dtype=bf16):
        return jax.ShapeDtypeStruct((rows, cols), dtype)

    def project(token_set, weights):
        count = weights.shape[1] // head_size
        outs = (shape(block, width), shape(block, count * head_size)) + (shape(block, head_size),) * count
        return vmem_call(project_kernel, (table,), (*token_set, weights), outs)

    normed_own, slope_own, up_part, value_own, query, key_own = project(own_set, w_in)
    near = over(jnp.where(odd, far, tokens), "seq", 2)
    far_other = over(far, "col", 1)
    far_set = (far, far_other, over(lax.optimization_barrier((far, query))[0], "seq", 1), over(far_other, "seq", 1))
    near_other = over(near, "col", 1)
    near_set = (near, near_other, over(near, "seq", 1), over(near_other, "seq", 1))
    cot_other = over(cotangent, "col", 1)
    cot_set = (cotangent, cot_other, over(cotangent, "seq", 1), over(cot_other, "seq", 1))

    normed_far, slope_far, value_far, key_far = project(far_set, w_kv)
    normed_near, slope_near, value_near, key_near = project(near_set, w_kv)
    keys = [key_far, key_near, key_own]
    values = [value_far, value_near, value_own]

    def forward(which, before):
        arrays = [query, keys[which], values[which], id_row]
        aliases = {}
        if before is not None:
            aliases = {3 + len(arrays): 0}
            arrays.append(before)
        return vmem_call(
            forward_kernel,
            tables,
            arrays,
            shape(block, head_size, f32),
            aliases,
            block_off=which * tiles,
            query_off=2 * tiles,
            scale=scale,
        )

    attended = forward(2, None)
    attended = forward(0, attended)
    attended = forward(1, attended)

    grad_narrow, gated, pre_up = vmem_call(
        middle_kernel,
        (table,),
        (attended, up_part, slope_own, *cot_set, w_out),
        (shape(block, head_size),) * 3,
    )
    out_send, out_keep, grad_early = vmem_call(
        outer_kernel,
        (table,),
        (gated, pre_up, normed_own, *cot_set, w_out),
        (shape(row_count, width), shape(row_count, width), shape(width, 2 * head_size, f32)),
    )

    def over_heads(send, keep):
        keep = keep.astype(f32) + over(send, "seq", 1).astype(f32)
        return keep[:, :half_width] + over(keep[:, half_width:].astype(bf16), "col", 1).astype(f32)

    def backward(which, weights, slope, before):
        arrays = [query, grad_narrow, keys[which], values[which], id_row, weights, slope, *before]
        outs = (
            shape(row_count, width),
            shape(row_count, width),
            shape(block, weights.shape[1]),
            shape(block, head_size, f32),
        )
        return vmem_call(
            backward_kernel,
            (*tables, table),
            arrays,
            outs,
            {4 + 7: 3} if before else None,
            scratch=[pltpu.VMEM((block, head_size), f32)] * 2,
            block_off=which * tiles,
            query_off=2 * tiles,
            scale=scale,
        )

    kv_shape = shape(width, 2 * head_size, f32)
    near_send, near_keep, near_grads, grad_query = backward(1, w_kv, slope_near, ())
    grad_kv = vmem_call(weight_kernel, (), (normed_near, near_grads), kv_shape)
    near_part = over_heads(near_send, near_keep)
    near_back = over(near_part.astype(bf16), "seq", 2).astype(f32)
    far_send, far_keep, far_grads, grad_query = backward(0, w_kv, slope_far, (grad_query,))
    grad_kv = vmem_call(weight_kernel, (), (normed_far, far_grads, grad_kv), kv_shape)
    far_part = over_heads(far_send, far_keep) + jnp.where(odd, near_back, 0.0)
    far_back = shift(far_part.astype(bf16), "seq", -4).astype(f32)
    own_send, own_keep, own_grads, _ = backward(2, w_in, slope_own, (grad_query, pre_up))
    own_part = over_heads(own_send, own_keep)
    grad_normed = own_part + jnp.where(odd, 0.0, near_back) + far_back
    out = (tokens.astype(f32) + over_heads(out_send, out_keep)).astype(bf16)

    lanes = 5 * head_size
    size = half_width
    sent, kept = vmem_call(
        weight_own_kernel,
        (table,),
        (normed_own, own_grads, grad_early, grad_kv),
        (shape(size, lanes), shape(size, lanes, f32)),
        scratch=[pltpu.VMEM((width, lanes), f32)],
    )
    for i, bit in enumerate(bits):
        received = over(sent, "seq", bit)
        if i + 1 < len(bits):
            size = size // 2
            sent, kept = vmem_call(
                halve_kernel,
                (table,),
                (kept, received),
                (shape(size, lanes), shape(size, lanes, f32)),
                step=i + 1,
            )
        else:
            total = vmem_call(last_kernel, (), (kept, received), shape(size, lanes))
    for i, bit in reversed(list(enumerate(bits))):
        total = jnp.concatenate([total, over(total, "seq", bit)], axis=0)

    grad_weight_in, grad_weight_out = vmem_call(
        assemble_kernel,
        (table,),
        (total, over(total, "seq", 1)),
        (shape(8 * width, head_size, f32), jax.ShapeDtypeStruct((2, head_size, width), f32)),
        scratch=[pltpu.VMEM((width, head_size), f32)],
        scale=1.0 / math.sqrt(row_count * seq_count),
        blocks=1 << steps,
    )
    grad_weight_in = grad_weight_in.reshape(width, 4, 2, head_size)

    own_wide = jnp.concatenate([tokens, own_other], axis=1).astype(f32)
    normed, inv_std = layer_norm(own_wide, epsilon)
    normed = normed[:, :half_width]
    sums = jnp.stack([jnp.sum(grad_normed, axis=1), jnp.sum(grad_normed * normed, axis=1)])
    sums = (sums + over(sums, "col", 1)) / width
    grad_tokens = inv_std * (grad_normed - sums[0][:, None] - normed * sums[1][:, None])
    grad_tokens = (grad_tokens + cotangent.astype(f32)).astype(bf16)
    return (out, grad_tokens, grad_weight_in, grad_weight_out)


def solution(mesh):
    placed = (
        P("seq", "col"),
        P("seq", "col"),
        P(None, None, "col", None),
        P("col", None, None),
        P(),
    )
    return jax.shard_map(
        layer,
        mesh=mesh,
        in_specs=placed,
        out_specs=(
            P("seq", "col"),
            P("seq", "col"),
            P(None, None, "col", None),
            P("col", None, None),
        ),
        check_vma=False,
    )
```
